128 devices in a mesh: va: 8 (over x, z_hi), vb: 8 (over z_lo, y), pair: 2 (over core).
Axes of the slice: x: 4, y: 4, z: 4 (z_hi: 2, z_lo: 2; z = z_hi * 2 + z_lo), core: 2. Of those that a mesh axis runs over, the one named last changes fastest.
Arguments:
- left_fit: bfloat16 [30, 2048, 1536], P('pair', 'va'), may hold values from -0.5 to 0.5
- right_fit: bfloat16 [30, 2048, 1536], P('pair', 'vb'), may hold values from -0.5 to 0.5
- occ_energy: float32 [8], replicated, may hold values from -1.5 to -0.3
- virt_energy: float32 [2048], replicated, may hold values from 0.2 to 2
- pair_list: int32 [30, 2], P('pair'), may hold values from 0 to 7, as said below
- domain_blocks: int32 [30, 12], P('pair'), may hold values from 0 to 31, as said below
Outputs:
- density: float32 [4096, 8, 2048], P(('vb', 'pair'), None, 'va')
The draws below stay inside these ranges and needn't reach their ends.
Inputs may be any that keep to these rules, and one draw needn't show every extreme that they name: `domain_blocks`: the 12 entries of a row are distinct. `pair_list`: each row holds two orbitals i <= j, and no two rows are the same pair.
All inputs are finite; a program needn't handle non-finite values.
Results may differ from the reference program's by a relative error of at most 0.0028.
Values may be sent and summed in bfloat16 or wider, within the bound.
No kernel may reach another device: no remote copies, remote signals or barrier semaphores. Data moves between devices by JAX's collectives and lax.ppermute only.
A program may use at most 192 MiB of HBM per device.

```python
import jax
import jax.numpy as jnp
from jax import lax

V = 2048
BLOCK = 128
DOM_BLK = 12
NOCC = 8
AUX_BLK = 32
DOM = 1536
PAIRS = 30


def draw_domain_blocks(key, part):
    row_keys = jax.random.split(key, PAIRS)

    def pick_row(row_key):
        return jax.random.permutation(row_key, AUX_BLK)[:DOM_BLK]
    chosen = jax.vmap(pick_row)(row_keys)
    return chosen.astype(jnp.int32)


def draw_pair_list(key, part):
    square = NOCC * NOCC
    flat_cells = jnp.arange(square, dtype=jnp.int32)
    first_orb = flat_cells // NOCC
    second_orb = flat_cells % NOCC
    rank_keys = jax.random.permutation(jax.random.fold_in(key, 17), square).astype(jnp.int32)
    rank_keys = jnp.where(first_orb <= second_orb, rank_keys, rank_keys + square)
    rank_keys = jnp.where((first_orb == 0) & (second_orb == NOCC - 1), -1, rank_keys)
    picked = jnp.argsort(rank_keys, stable=True)[:PAIRS]
    return jnp.stack([first_orb[picked], second_orb[picked]], axis=1).astype(jnp.int32)


def steps_of(rng, shape, cuts, least, largest):
    def one(axis_at, blocks):
        draws = jax.random.uniform(jax.random.fold_in(jax.random.fold_in(rng, 6), axis_at), (blocks,), jnp.float32, least / len(cuts), largest / len(cuts))
        return jnp.repeat(jnp.exp(draws), shape[axis_at] // blocks).reshape((-1,) + (1,) * (len(shape) - axis_at - 1))

    loudness = one(*cuts[0])
    for cut in cuts[1:]:
        loudness = loudness * one(*cut)
    return loudness


def centred(rng, extent, scale, bound, cuts=(), kind=jnp.bfloat16):
    entries = scale * jax.random.normal(rng, extent, jnp.float32)
    if cuts:
        entries = entries * steps_of(rng, extent, cuts, -0.22, 0.18)
    return jnp.clip(entries, -bound, bound).astype(kind)


def setup_inputs(seed: int = 0) -> dict:
    key_list = jax.random.split(jax.random.key(seed), 7)
    return {
        "left_fit": centred(key_list[0], (PAIRS, V, DOM), 0.08, 0.5, ((0, 2), (1, 8))),
        "right_fit": centred(key_list[1], (PAIRS, V, DOM), 0.08, 0.5, ((0, 2), (1, 8))),
        "occ_energy": jnp.clip(jax.random.uniform(key_list[2], (NOCC,), jnp.float32, -1.5, -0.3), -1.5, -0.3),
        "virt_energy": jnp.clip(jax.random.uniform(key_list[3], (V,), jnp.float32, 0.2, 2.0), 0.2, 2.0),
        "pair_list": draw_pair_list(jax.random.fold_in(key_list[6], 71), 0),
        "domain_blocks": draw_domain_blocks(jax.random.fold_in(key_list[6], 71), 0),
    }


def reference(left_fit, right_fit, occ_energy, virt_energy, pair_list, domain_blocks):
    total_pairs = left_fit.shape[0]

    def one_pair(running, pair_index):
        left_rows = left_fit[pair_index]
        right_rows = right_fit[pair_index]
        coulomb = jnp.dot(left_rows, right_rows.T, preferred_element_type=jnp.float32).astype(jnp.bfloat16)
        first_occ = pair_list[pair_index, 0]
        second = pair_list[pair_index, 1]
        energy_gap = virt_energy[:, None] + virt_energy[None, :] - occ_energy[first_occ] - occ_energy[second]
        coulomb_wide = coulomb.astype(jnp.float32)
        amplitude = ((2.0 * coulomb_wide - coulomb_wide.T) / energy_gap).astype(jnp.bfloat16)
        contracted = jnp.dot(right_rows.T, amplitude.T, preferred_element_type=jnp.float32)
        pieces = contracted.reshape(DOM_BLK, BLOCK, V)
        running = running.at[domain_blocks[pair_index], first_occ].add(pieces)
        return running, None

    zero_dense = jnp.zeros((AUX_BLK, NOCC, BLOCK, V), jnp.float32)
    accumulated, unused = lax.scan(one_pair, zero_dense, jnp.arange(total_pairs, dtype=jnp.int32))
    return accumulated.transpose(0, 2, 1, 3).reshape(AUX_BLK * BLOCK, NOCC, V)
```

```python
import itertools

import jax
import jax.numpy as jnp
from jax import lax
from jax.experimental import pallas as pl
from jax.experimental.pallas import tpu as pltpu
from jax.sharding import PartitionSpec as P

BLOCK = 128
NOCC = 8
AUX_BLK = 32
CHUNKS = 5
AXES = ("va", "vb", "pair")
DETOURS = (
    (1, 0, 3), (0, 2, 0), (1, 0, 0), (2, 1, 0), (2, 2, 2),
    (3, 0, 2), (0, 3, 1), (3, 3, 1), (1, 1, 1), (3, 1, 3),
)


def to_flat(x, y, z, core):
    va = x * 2 + z // 2
    vb = (z % 2) * 4 + y
    return (va * 8 + vb) * 2 + core


def mirror_chip(x, y, z):
    va, vb = x * 2 + z // 2, (z % 2) * 4 + y
    va, vb = vb, va
    return va // 2, vb % 4, (va % 2) * 2 + vb // 4


def detour_pairs(piece):
    out, back = [], []
    for x, y, z, core in itertools.product(range(4), range(4), range(4), range(2)):
        dx, dy, dz = DETOURS[core * CHUNKS + piece]
        mid = ((x + dx) % 4, (y + dy) % 4, (z + dz) % 4)
        out.append((to_flat(x, y, z, core), to_flat(*mid, core)))
        back.append((to_flat(*mid, core), to_flat(*mirror_chip(x, y, z), core)))
    return out, back


def coulomb_kernel(left_ref, right_ref, out_ref):
    out_ref[0] = lax.dot_general(
        left_ref[0], right_ref[0], (((1,), (1,)), ((), ())), preferred_element_type=jnp.float32
    ).astype(jnp.bfloat16)


def coulomb_chunk(left_fit, right_fit, start, count):
    _, rows, dom = left_fit.shape
    spec = pl.BlockSpec((1, rows, dom), lambda p: (p + start, 0, 0))
    return pl.pallas_call(
        coulomb_kernel,
        grid=(count,),
        in_specs=[spec, spec],
        out_specs=pl.BlockSpec((1, rows, rows), lambda p: (p, 0, 0)),
        out_shape=jax.ShapeDtypeStruct((count, rows, rows), jnp.bfloat16),
        cost_estimate=pl.CostEstimate(
            flops=2 * count * rows * rows * dom,
            bytes_accessed=4 * count * rows * dom + 2 * count * rows * rows,
            transcendentals=0,
        ),
        name="coulomb",
    )(left_fit, right_fit)


def amplitude_kernel(chunks, *refs):
    core_ref, occ_ref, pair_ref, ea_ref, eb_ref = refs[:5]
    tiles = refs[5 : 5 + chunks]
    mirrors = refs[5 + chunks : 5 + 2 * chunks]
    keep_ref, send_ref, work_ref = refs[5 + 2 * chunks :]
    half = keep_ref.shape[1]
    count = tiles[0].shape[0]
    core = core_ref[0]
    base = ea_ref[...] + eb_ref[...]
    mine = pl.multiple_of(core * half, half)
    other = pl.multiple_of((1 - core) * half, half)
    for chunk in range(chunks):
        for row in range(count):
            p = chunk * count + row
            gap = base - occ_ref[pair_ref[p, 0]] - occ_ref[pair_ref[p, 1]]
            tile = tiles[chunk][row].astype(jnp.float32)
            swapped = mirrors[chunk][row].astype(jnp.float32).T
            work_ref[p % 2] = ((2.0 * tile - swapped) / gap).astype(jnp.bfloat16)
            keep_ref[p] = work_ref[p % 2, pl.ds(mine, half), :]
            send_ref[p] = work_ref[p % 2, pl.ds(other, half), :]


def amplitude(core, occ_energy, pair_list, ea, eb, tiles, mirrors):
    pairs = pair_list.shape[0]
    rows = tiles[0].shape[1]
    smem = pl.BlockSpec(memory_space=pltpu.SMEM)
    vmem = pl.BlockSpec(memory_space=pltpu.VMEM)
    chunks = len(tiles)
    shape = jax.ShapeDtypeStruct((pairs, rows // 2, rows), jnp.bfloat16)
    return pl.pallas_call(
        lambda *refs: amplitude_kernel(chunks, *refs),
        in_specs=[smem] * 3 + [vmem] * (2 + 2 * chunks),
        out_specs=[vmem, vmem],
        out_shape=[shape, shape],
        scratch_shapes=[pltpu.VMEM((2, rows, rows), jnp.bfloat16)],
        cost_estimate=pl.CostEstimate(
            flops=10 * pairs * rows * rows, bytes_accessed=6 * pairs * rows * rows, transcendentals=0
        ),
        name="amplitude",
    )(core, occ_energy, pair_list, ea.reshape(rows, 1), eb.reshape(1, rows), *tiles, *mirrors)


def contract_kernel(pairs, dom_blocks, slot_ref, amp0, amp1, right0, right1, out_ref, acc_ref):
    step = pl.program_id(0)

    @pl.when(step == 0)
    def _():
        acc_ref[...] = jnp.zeros_like(acc_ref)

    @pl.when(step < pairs)
    def _():
        for side, (amp, right) in enumerate(((amp0, right0), (amp1, right1))):
            part = jnp.dot(amp[0], right[0], preferred_element_type=jnp.float32)
            for k in range(dom_blocks):
                slot = slot_ref[side, step, k]
                acc_ref[slot] += part[:, k * BLOCK : (k + 1) * BLOCK]

    @pl.when(step >= pairs)
    def _():
        group = out_ref.shape[0]
        start = pl.multiple_of((step - pairs) * group, group)
        out_ref[...] = acc_ref[pl.ds(start, group)].astype(out_ref.dtype)


def contract(slots, amp0, amp1, right0, right1, dom_blocks):
    pairs, half, rows = amp0.shape
    dom = right0.shape[2]
    total = AUX_BLK * NOCC
    group = 16
    amp_spec = pl.BlockSpec((1, half, rows), lambda s, t: (jnp.minimum(s, pairs - 1), 0, 0))
    right_spec = pl.BlockSpec((1, rows, dom), lambda s, t: (jnp.minimum(s, pairs - 1), 0, 0))
    return pl.pallas_call(
        lambda *refs: contract_kernel(pairs, dom_blocks, *refs),
        grid_spec=pltpu.PrefetchScalarGridSpec(
            num_scalar_prefetch=1,
            grid=(pairs + total // group,),
            in_specs=[amp_spec, amp_spec, right_spec, right_spec],
            out_specs=pl.BlockSpec(
                (group, half, BLOCK), lambda s, t: (jnp.maximum(s - pairs, 0), 0, 0)
            ),
            scratch_shapes=[pltpu.VMEM((total, half, BLOCK), jnp.float32)],
        ),
        out_shape=jax.ShapeDtypeStruct((total, half, BLOCK), jnp.bfloat16),
        cost_estimate=pl.CostEstimate(
            flops=4 * pairs * half * rows * dom,
            bytes_accessed=4 * pairs * rows * dom + 2 * total * half * BLOCK,
            transcendentals=0,
        ),
        name="contract",
    )(slots, amp0, amp1, right0, right1)


def collect_kernel(in_ref, out_ref):
    sources = in_ref.shape[0]
    half = in_ref.shape[3]
    for occ in range(NOCC):
        for core in range(2):
            total = in_ref[core, 0, occ].astype(jnp.float32)
            for source in range(2 + core, sources, 2):
                total = total + in_ref[source, 0, occ].astype(jnp.float32)
            out_ref[:, occ, core * half : (core + 1) * half] = total.T


def collect(parts):
    sources, blocks, _, half, _ = parts.shape
    return pl.pallas_call(
        collect_kernel,
        grid=(blocks,),
        in_specs=[
            pl.BlockSpec((sources, 1, NOCC, half, BLOCK), lambda b: (0, b, 0, 0, 0))
        ],
        out_specs=pl.BlockSpec((BLOCK, NOCC, 2 * half), lambda b: (b, 0, 0)),
        out_shape=jax.ShapeDtypeStruct((blocks * BLOCK, NOCC, 2 * half), jnp.float32),
        cost_estimate=pl.CostEstimate(
            flops=parts.size, bytes_accessed=2 * parts.size, transcendentals=0
        ),
        name="collect",
    )(parts)


def shards(left_fit, right_fit, occ_energy, virt_energy, pair_list, domain_blocks):
    pairs, rows, _ = left_fit.shape
    dom_blocks = domain_blocks.shape[1]
    core = lax.axis_index("pair")
    ea = lax.dynamic_slice_in_dim(virt_energy, lax.axis_index("va") * rows, rows)
    eb = lax.dynamic_slice_in_dim(virt_energy, lax.axis_index("vb") * rows, rows)
    swap = [(0, 1), (1, 0)]
    slots = domain_blocks * NOCC + pair_list[:, :1]
    other_slots = lax.ppermute(slots, "pair", swap)
    other_right = lax.ppermute(right_fit, "pair", swap)
    count = pairs // CHUNKS
    tiles, mirrors = [], []
    for piece in range(CHUNKS):
        tile = coulomb_chunk(left_fit, right_fit, piece * count, count)
        out, back = detour_pairs(piece)
        mid = lax.ppermute(tile, AXES, out)
        mirrors.append(lax.ppermute(mid, AXES, back))
        tiles.append(tile)
    keep, send = amplitude(
        core.reshape(1).astype(jnp.int32), occ_energy, pair_list, ea, eb, tiles, mirrors
    )
    other_amp = lax.ppermute(send, "pair", swap)
    sums = contract(
        jnp.stack([slots, other_slots]), keep, other_amp, right_fit, other_right, dom_blocks
    )
    owners = lax.axis_size("vb") * lax.axis_size("pair")
    parts = sums.reshape(owners, -1, rows // 2, BLOCK)
    parts = lax.all_to_all(parts, ("vb", "pair"), split_axis=0, concat_axis=0, tiled=True)
    return collect(parts.reshape(owners, -1, NOCC, rows // 2, BLOCK))


def solution(mesh):
    return jax.shard_map(
        shards,
        mesh=mesh,
        in_specs=(
            P("pair", "va", None),
            P("pair", "vb", None),
            P(),
            P(),
            P("pair", None),
            P("pair", None),
        ),
        out_specs=P(("vb", "pair"), None, "va"),
        check_vma=False,
    )
```

```python
import itertools

import jax
import jax.numpy as jnp
from jax import lax
from jax.experimental import pallas as pl
from jax.experimental.pallas import tpu as pltpu
from jax.sharding import PartitionSpec as P

BLOCK = 128
NOCC = 8
AUX_BLK = 32
CHUNKS = 5
SPLIT = 4
PER_OWNER = 4
AXES = ("va", "vb", "pair")
DETOURS = (
    (1, 0, 3), (0, 2, 0), (1, 0, 0), (2, 1, 0), (2, 2, 2),
    (3, 0, 2), (0, 3, 1), (3, 3, 1), (1, 1, 1), (3, 1, 3),
)


def to_flat(x, y, z, core):
    va = x * 2 + z // 2
    vb = (z % 2) * 4 + y
    return (va * 8 + vb) * 2 + core


def mirror_chip(x, y, z):
    va, vb = x * 2 + z // 2, (z % 2) * 4 + y
    va, vb = vb, va
    return va // 2, vb % 4, (va % 2) * 2 + vb // 4


def detour_pairs(piece):
    out, back = [], []
    for x, y, z, core in itertools.product(range(4), range(4), range(4), range(2)):
        dx, dy, dz = DETOURS[core * CHUNKS + piece]
        mid = ((x + dx) % 4, (y + dy) % 4, (z + dz) % 4)
        out.append((to_flat(x, y, z, core), to_flat(*mid, core)))
        back.append((to_flat(*mid, core), to_flat(*mirror_chip(x, y, z), core)))
    return out, back


def coulomb_kernel(left_ref, right_ref, out_ref):
    out_ref[0] = lax.dot_general(
        left_ref[0], right_ref[0], (((1,), (1,)), ((), ())), preferred_element_type=jnp.float32
    ).astype(jnp.bfloat16)


def coulomb_chunk(left_fit, right_fit, start, count):
    _, rows, dom = left_fit.shape
    spec = pl.BlockSpec((1, rows, dom), lambda p: (p + start, 0, 0))
    return pl.pallas_call(
        coulomb_kernel,
        grid=(count,),
        in_specs=[spec, spec],
        out_specs=pl.BlockSpec((1, rows, rows), lambda p: (p, 0, 0)),
        out_shape=jax.ShapeDtypeStruct((count, rows, rows), jnp.bfloat16),
        cost_estimate=pl.CostEstimate(
            flops=2 * count * rows * rows * dom,
            bytes_accessed=4 * count * rows * dom + 2 * count * rows * rows,
            transcendentals=0,
        ),
        name="coulomb",
    )(left_fit, right_fit)


def amplitude_kernel(chunks, *refs):
    core_ref, occ_ref, pair_ref, ea_ref, eb_ref = refs[:5]
    tiles = refs[5 : 5 + chunks]
    mirrors = refs[5 + chunks : 5 + 2 * chunks]
    keep_ref, send_ref, work_ref = refs[5 + 2 * chunks :]
    half = keep_ref.shape[1]
    count = tiles[0].shape[0]
    core = core_ref[0]
    base = ea_ref[...] + eb_ref[...]
    mine = pl.multiple_of(core * half, half)
    other = pl.multiple_of((1 - core) * half, half)
    for chunk in range(chunks):
        for row in range(count):
            p = chunk * count + row
            gap = base - occ_ref[pair_ref[p, 0]] - occ_ref[pair_ref[p, 1]]
            tile = tiles[chunk][row].astype(jnp.float32)
            swapped = mirrors[chunk][row].astype(jnp.float32).T
            work_ref[p % 2] = ((2.0 * tile - swapped) / gap).astype(jnp.bfloat16)
            keep_ref[p] = work_ref[p % 2, pl.ds(mine, half), :]
            send_ref[p] = work_ref[p % 2, pl.ds(other, half), :]


def amplitude(core, occ_energy, pair_list, ea, eb, tiles, mirrors):
    pairs = pair_list.shape[0]
    rows = tiles[0].shape[1]
    smem = pl.BlockSpec(memory_space=pltpu.SMEM)
    vmem = pl.BlockSpec(memory_space=pltpu.VMEM)
    chunks = len(tiles)
    shape = jax.ShapeDtypeStruct((pairs, rows // 2, rows), jnp.bfloat16)
    return pl.pallas_call(
        lambda *refs: amplitude_kernel(chunks, *refs),
        in_specs=[smem] * 3 + [vmem] * (2 + 2 * chunks),
        out_specs=[vmem, vmem],
        out_shape=[shape, shape],
        scratch_shapes=[pltpu.VMEM((2, rows, rows), jnp.bfloat16)],
        cost_estimate=pl.CostEstimate(
            flops=10 * pairs * rows * rows, bytes_accessed=6 * pairs * rows * rows, transcendentals=0
        ),
        name="amplitude",
    )(core, occ_energy, pair_list, ea.reshape(rows, 1), eb.reshape(1, rows), *tiles, *mirrors)


def contract_kernel(pairs, dom_blocks, low, slot_ref, occ_ref, amp0, amp1, right0, right1, *refs):
    out_refs, acc_ref = refs[:-1], refs[-1]
    step = pl.program_id(0)
    high = low + SPLIT

    @pl.when(step == 0)
    def _():
        acc_ref[...] = jnp.zeros_like(acc_ref)

    for side, (amp, right) in enumerate(((amp0, right0), (amp1, right1))):
        place = jnp.minimum(step, pairs - 1)
        orbital = occ_ref[side, place]

        @pl.when((step < pairs) & (orbital >= low) & (orbital < high))
        def _():
            part = jnp.dot(amp[0], right[0], preferred_element_type=jnp.float32)
            for k in range(dom_blocks):
                slot = slot_ref[side, place, k] + orbital - low
                acc_ref[slot] += part[:, k * BLOCK : (k + 1) * BLOCK]

    @pl.when(step >= pairs)
    def _():
        group = out_refs[0].shape[1]
        offset = step - pairs
        blocks = out_refs[0].shape[0] * (pl.num_programs(0) - pairs)
        for index, out_ref in enumerate(out_refs):
            start = pl.multiple_of((index * blocks + offset) * group, group)
            out_ref[0] = acc_ref[pl.ds(start, group)].astype(out_ref.dtype)


def contract(slots, orbitals, amp0, amp1, right0, right1, dom_blocks, low, outs):
    pairs, half, rows = amp0.shape
    dom = right0.shape[2]
    total = AUX_BLK * SPLIT
    group = PER_OWNER * SPLIT
    blocks = total // group // outs
    amp_spec = pl.BlockSpec((1, half, rows), lambda s, *_: (jnp.minimum(s, pairs - 1), 0, 0))
    right_spec = pl.BlockSpec((1, rows, dom), lambda s, *_: (jnp.minimum(s, pairs - 1), 0, 0))
    return pl.pallas_call(
        lambda *refs: contract_kernel(pairs, dom_blocks, low, *refs),
        grid_spec=pltpu.PrefetchScalarGridSpec(
            num_scalar_prefetch=2,
            grid=(pairs + blocks,),
            in_specs=[amp_spec, amp_spec, right_spec, right_spec],
            out_specs=[
                pl.BlockSpec(
                    (1, group, half, BLOCK), lambda s, *_: (jnp.maximum(s - pairs, 0), 0, 0, 0)
                )
            ]
            * outs,
            scratch_shapes=[pltpu.VMEM((total, half, BLOCK), jnp.float32)],
        ),
        out_shape=[jax.ShapeDtypeStruct((blocks, group, half, BLOCK), jnp.bfloat16)] * outs,
        cost_estimate=pl.CostEstimate(
            flops=2 * pairs * half * rows * dom,
            bytes_accessed=4 * pairs * rows * dom + 2 * total * half * BLOCK,
            transcendentals=0,
        ),
        name="contract",
    )(slots, orbitals, amp0, amp1, right0, right1)


def add_kernel(terms, *refs):
    ins, outs = refs[:terms], refs[terms:]
    for index, out_ref in enumerate(outs):
        total = ins[0][index].astype(jnp.float32)
        for term in ins[1:]:
            total = total + term[index].astype(jnp.float32)
        out_ref[...] = total.astype(out_ref.dtype)


def add_split(arrays):
    pieces, group, half, width = arrays[0].shape
    tile = 4
    return pl.pallas_call(
        lambda *refs: add_kernel(len(arrays), *refs),
        grid=(group // tile,),
        in_specs=[pl.BlockSpec((pieces, tile, half, width), lambda g: (0, g, 0, 0))] * len(arrays),
        out_specs=[pl.BlockSpec((tile, half, width), lambda g: (g, 0, 0))] * pieces,
        out_shape=[
            jax.ShapeDtypeStruct((group, half, width), jnp.float32 if p == 0 else jnp.bfloat16)
            for p in range(pieces)
        ],
        cost_estimate=pl.CostEstimate(
            flops=len(arrays) * arrays[0].size,
            bytes_accessed=2 * (len(arrays) + 2) * arrays[0].size,
            transcendentals=0,
        ),
        name="add_split",
    )(*arrays)


def finish_kernel(core_ref, *refs):
    ins, (keep_ref, send_ref) = refs[:-2], refs[-2:]
    core = core_ref[0]
    per_core = PER_OWNER // 2
    for who, out_ref in ((core, keep_ref), (1 - core, send_ref)):
        for block in range(per_core):
            for occ in range(SPLIT):
                row = (who * per_core + block) * SPLIT + occ
                total = ins[0][row].astype(jnp.float32)
                for term in ins[1:]:
                    total = total + term[row].astype(jnp.float32)
                out_ref[occ, block * BLOCK : (block + 1) * BLOCK, :] = total.T


def finish(core, arrays):
    _, half, width = arrays[0].shape
    vmem = pl.BlockSpec(memory_space=pltpu.VMEM)
    shape = jax.ShapeDtypeStruct((SPLIT, PER_OWNER // 2 * width, half), jnp.float32)
    return pl.pallas_call(
        finish_kernel,
        in_specs=[pl.BlockSpec(memory_space=pltpu.SMEM)] + [vmem] * len(arrays),
        out_specs=[vmem, vmem],
        out_shape=[shape, shape],
        cost_estimate=pl.CostEstimate(
            flops=len(arrays) * arrays[0].size,
            bytes_accessed=2 * (len(arrays) + 3) * arrays[0].size,
            transcendentals=0,
        ),
        name="finish",
    )(core, *arrays)


def join_kernel(core_ref, *refs):
    ins, out_ref = refs[:-1], refs[-1]
    half = ins[0].shape[2]
    core = core_ref[0]

    def write(order):
        for part in range(len(ins) // 2):
            for occ in range(SPLIT):
                for side in range(2):
                    out_ref[:, part * SPLIT + occ, side * half : (side + 1) * half] = ins[
                        2 * part + (side if order == 0 else 1 - side)
                    ][occ]

    @pl.when(core == 0)
    def _():
        write(0)

    @pl.when(core != 0)
    def _():
        write(1)


def join(core, arrays):
    _, rows, half = arrays[0].shape
    parts = len(arrays) // 2
    tile = 64
    return pl.pallas_call(
        join_kernel,
        grid=(rows // tile,),
        in_specs=[pl.BlockSpec(memory_space=pltpu.SMEM)]
        + [pl.BlockSpec((SPLIT, tile, half), lambda r: (0, r, 0))] * len(arrays),
        out_specs=pl.BlockSpec((tile, parts * SPLIT, 2 * half), lambda r: (r, 0, 0)),
        out_shape=jax.ShapeDtypeStruct((rows, parts * SPLIT, 2 * half), jnp.float32),
        cost_estimate=pl.CostEstimate(
            flops=0, bytes_accessed=16 * parts * SPLIT * rows * half, transcendentals=0
        ),
        name="join",
    )(core, *arrays)


def shift_y(value, by):
    pairs = [(z * 4 + y, z * 4 + (y + by) % 4) for z in range(2) for y in range(4)]
    return lax.ppermute(value, "vb", pairs)


def swap_z(value):
    return lax.ppermute(value, "vb", [(j, (j + 4) % 8) for j in range(8)])


def shards(left_fit, right_fit, occ_energy, virt_energy, pair_list, domain_blocks):
    pairs, rows, _ = left_fit.shape
    dom_blocks = domain_blocks.shape[1]
    core = lax.axis_index("pair")
    ea = lax.dynamic_slice_in_dim(virt_energy, lax.axis_index("va") * rows, rows)
    eb = lax.dynamic_slice_in_dim(virt_energy, lax.axis_index("vb") * rows, rows)
    swap = [(0, 1), (1, 0)]
    vb = lax.axis_index("vb")
    table = jnp.concatenate([domain_blocks, pair_list[:, :1]], axis=1)
    other = lax.ppermute(table, "pair", swap)
    both = jnp.stack([table, other])
    blocks, orbitals = both[:, :, :dom_blocks], both[:, :, dom_blocks]
    apart_z = (blocks // PER_OWNER // 4 - vb // 4) % 2
    apart_y = (blocks // PER_OWNER - vb) % 4
    inner = blocks % PER_OWNER
    slots_zy = ((apart_z * 4 + apart_y) * PER_OWNER + inner) * SPLIT
    slots_yz = ((apart_y * 2 + apart_z) * PER_OWNER + inner) * SPLIT
    other_right = lax.ppermute(right_fit, "pair", swap)
    count = pairs // CHUNKS
    tiles, mirrors = [], []
    for piece in range(CHUNKS):
        tile = coulomb_chunk(left_fit, right_fit, piece * count, count)
        out, back = detour_pairs(piece)
        mid = lax.ppermute(tile, AXES, out)
        mirrors.append(lax.ppermute(mid, AXES, back))
        tiles.append(tile)
    me = core.reshape(1).astype(jnp.int32)
    keep, send = amplitude(me, occ_energy, pair_list, ea, eb, tiles, mirrors)
    other_amp = lax.ppermute(send, "pair", swap)
    operands = (orbitals, keep, other_amp, right_fit, other_right, dom_blocks)
    stay, cross = contract(slots_zy, *operands, SPLIT, 2)
    crossed = swap_z(cross)
    beside = contract(slots_yz, *operands, 0, 4)
    moved = [shift_y(beside[by], by) for by in (1, 3, 2)]
    first = add_split([stay, crossed])
    late = [shift_y(first[by], by) for by in (1, 3, 2)]
    second = add_split([beside[0], *moved])
    far = swap_z(second[1])
    keep1, send1 = finish(me, [first[0], *late])
    got1 = lax.ppermute(send1, "pair", swap)
    keep0, send0 = finish(me, [second[0], far])
    got0 = lax.ppermute(send0, "pair", swap)
    return join(me, [keep0, got0, keep1, got1])


def solution(mesh):
    return jax.shard_map(
        shards,
        mesh=mesh,
        in_specs=(
            P("pair", "va", None),
            P("pair", "vb", None),
            P(),
            P(),
            P("pair", None),
            P("pair", None),
        ),
        out_specs=P(("vb", "pair"), None, "va"),
        check_vma=False,
    )
```

```python
import itertools

import jax
import jax.numpy as jnp
from jax import lax
from jax.experimental import pallas as pl
from jax.experimental.pallas import tpu as pltpu
from jax.sharding import PartitionSpec as P

BLOCK = 128
NOCC = 8
AUX_BLK = 32
CHUNKS = 5
SPLIT = 4
PER_OWNER = 4
AXES = ("va", "vb", "pair")
DETOURS = (
    (1, 0, 3), (0, 2, 0), (1, 0, 0), (2, 1, 0), (2, 2, 2),
    (3, 0, 2), (0, 3, 1), (3, 3, 1), (1, 1, 1), (3, 1, 3),
)


def to_flat(x, y, z, core):
    va = x * 2 + z // 2
    vb = (z % 2) * 4 + y
    return (va * 8 + vb) * 2 + core


def mirror_chip(x, y, z):
    va, vb = x * 2 + z // 2, (z % 2) * 4 + y
    va, vb = vb, va
    return va // 2, vb % 4, (va % 2) * 2 + vb // 4


def detour_pairs(piece):
    out, back = [], []
    for x, y, z, core in itertools.product(range(4), range(4), range(4), range(2)):
        dx, dy, dz = DETOURS[core * CHUNKS + piece]
        mid = ((x + dx) % 4, (y + dy) % 4, (z + dz) % 4)
        out.append((to_flat(x, y, z, core), to_flat(*mid, core)))
        back.append((to_flat(*mid, core), to_flat(*mirror_chip(x, y, z), core)))
    return out, back


def coulomb_kernel(start, chunks, left_ref, right_ref, *refs):
    out_refs, (left_buf, right_buf, sems) = refs[-3 - chunks : -3], refs[-3:]
    count = out_refs[0].shape[0]
    copies = []
    for p in range(count * len(out_refs)):
        pair = [
            pltpu.make_async_copy(left_ref.at[start + p], left_buf.at[p], sems.at[0, p]),
            pltpu.make_async_copy(right_ref.at[start + p], right_buf.at[p], sems.at[1, p]),
        ]
        for copy in pair:
            copy.start()
        copies.append(pair)
    for p, pair in enumerate(copies):
        for copy in pair:
            copy.wait()
        out_refs[p // count][p % count] = lax.dot_general(
            left_buf[p], right_buf[p], (((1,), (1,)), ((), ())), preferred_element_type=jnp.float32
        ).astype(jnp.bfloat16)


def coulomb(left_fit, right_fit, start, count, chunks, after=()):
    _, rows, dom = left_fit.shape
    total = count * chunks
    hbm = pl.BlockSpec(memory_space=pl.ANY)
    return pl.pallas_call(
        lambda *refs: coulomb_kernel(start, chunks, *refs),
        in_specs=[hbm] * (2 + len(after)),
        out_specs=[pl.BlockSpec(memory_space=pltpu.VMEM)] * chunks,
        out_shape=[jax.ShapeDtypeStruct((count, rows, rows), jnp.bfloat16)] * chunks,
        scratch_shapes=[
            pltpu.VMEM((total, rows, dom), jnp.bfloat16),
            pltpu.VMEM((total, rows, dom), jnp.bfloat16),
            pltpu.SemaphoreType.DMA((2, total)),
        ],
        cost_estimate=pl.CostEstimate(
            flops=2 * total * rows * rows * dom,
            bytes_accessed=4 * total * rows * dom + 2 * total * rows * rows,
            transcendentals=0,
        ),
        compiler_params=pltpu.CompilerParams(vmem_limit_bytes=40 << 20),
        name="coulomb",
    )(left_fit, right_fit, *after)


def amplitude_kernel(chunks, *refs):
    core_ref, occ_ref, pair_ref = refs[:3]
    keep_ref, send_ref, work_ref = refs[-3:]
    ea_ref, eb_ref = refs[-5 - 2 * chunks : -3 - 2 * chunks]
    tiles = refs[-3 - 2 * chunks : -3 - chunks]
    mirrors = refs[-3 - chunks : -3]
    half = keep_ref.shape[1]
    count = tiles[0].shape[0]
    core = core_ref[0]
    base = ea_ref[...] + eb_ref[...]
    mine = pl.multiple_of(core * half, half)
    other = pl.multiple_of((1 - core) * half, half)
    for chunk in range(chunks):
        for row in range(count):
            p = chunk * count + row
            gap = base - occ_ref[pair_ref[p, 0]] - occ_ref[pair_ref[p, 1]]
            tile = tiles[chunk][row].astype(jnp.float32)
            swapped = mirrors[chunk][row].astype(jnp.float32).T
            work_ref[p % 2] = ((2.0 * tile - swapped) / gap).astype(jnp.bfloat16)
            keep_ref[p] = work_ref[p % 2, pl.ds(mine, half), :]
            send_ref[p] = work_ref[p % 2, pl.ds(other, half), :]


def amplitude(core, occ_energy, pair_list, ea, eb, tiles, mirrors, ready):
    pairs = pair_list.shape[0]
    rows = tiles[0].shape[1]
    smem = pl.BlockSpec(memory_space=pltpu.SMEM)
    vmem = pl.BlockSpec(memory_space=pltpu.VMEM)
    chunks = len(tiles)
    shape = jax.ShapeDtypeStruct((pairs, rows // 2, rows), jnp.bfloat16)
    return pl.pallas_call(
        lambda *refs: amplitude_kernel(chunks, *refs),
        in_specs=[smem] * (3 + len(ready)) + [vmem] * (2 + 2 * chunks),
        out_specs=[vmem, vmem],
        out_shape=[shape, shape],
        scratch_shapes=[pltpu.VMEM((2, rows, rows), jnp.bfloat16)],
        cost_estimate=pl.CostEstimate(
            flops=10 * pairs * rows * rows, bytes_accessed=6 * pairs * rows * rows, transcendentals=0
        ),
        name="amplitude",
    )(
        core, occ_energy, pair_list, *ready, ea.reshape(rows, 1), eb.reshape(1, rows), *tiles, *mirrors
    )


def contract_kernel(low, slot_ref, occ_ref, amp0, amp1, right0, right1, *refs):
    out_refs, (buf_ref, acc_ref, stage_ref, in_sems, out_sems) = refs[:-5], refs[-5:]
    pairs = amp0.shape[0]
    dom_blocks = slot_ref.shape[2]
    sides = ((amp0, right0), (amp1, right1))

    def taken(side, p):
        return (occ_ref[side, p] >= low) & (occ_ref[side, p] < low + SPLIT)

    def load(side, p):
        return pltpu.make_async_copy(
            sides[side][1].at[p], buf_ref.at[side, p], in_sems.at[side, p]
        )

    for side in range(2):

        @pl.loop(0, pairs)
        def _(p):
            @pl.when(taken(side, p))
            def _():
                load(side, p).start()

    acc_ref[...] = jnp.zeros_like(acc_ref)
    for side in range(2):

        @pl.loop(0, pairs)
        def _(p):
            @pl.when(taken(side, p))
            def _():
                load(side, p).wait()
                part = jnp.dot(sides[side][0][p], buf_ref[side, p], preferred_element_type=jnp.float32)
                for k in range(dom_blocks):
                    slot = slot_ref[side, p, k] + occ_ref[side, p] - low
                    acc_ref[slot] += part[:, k * BLOCK : (k + 1) * BLOCK]

    group = out_refs[0].shape[1]
    copies = []
    for out_ref in out_refs:
        for block in range(out_ref.shape[0]):
            place = len(copies)
            stage_ref[place] = acc_ref[place * group : (place + 1) * group].astype(stage_ref.dtype)
            copy = pltpu.make_async_copy(
                stage_ref.at[place], out_ref.at[block], out_sems.at[place]
            )
            copy.start()
            copies.append(copy)
    for copy in copies:
        copy.wait()


def contract(slots, orbitals, amp0, amp1, right0, right1, low, outs):
    pairs, half, rows = amp0.shape
    dom = right0.shape[2]
    total = AUX_BLK * SPLIT
    places = sum(outs)
    group = total // places
    smem = pl.BlockSpec(memory_space=pltpu.SMEM)
    vmem = pl.BlockSpec(memory_space=pltpu.VMEM)
    hbm = pl.BlockSpec(memory_space=pl.ANY)
    return pl.pallas_call(
        lambda *refs: contract_kernel(low, *refs),
        in_specs=[smem, smem, vmem, vmem, hbm, hbm],
        out_specs=[hbm] * len(outs),
        out_shape=[jax.ShapeDtypeStruct((n, group, half, BLOCK), jnp.bfloat16) for n in outs],
        scratch_shapes=[
            pltpu.VMEM((2, pairs, rows, dom), jnp.bfloat16),
            pltpu.VMEM((total, half, BLOCK), jnp.float32),
            pltpu.VMEM((places, group, half, BLOCK), jnp.bfloat16),
            pltpu.SemaphoreType.DMA((2, pairs)),
            pltpu.SemaphoreType.DMA((places,)),
        ],
        cost_estimate=pl.CostEstimate(
            flops=2 * pairs * half * rows * dom,
            bytes_accessed=2 * pairs * rows * dom + 2 * total * half * BLOCK,
            transcendentals=0,
        ),
        compiler_params=pltpu.CompilerParams(vmem_limit_bytes=60 << 20),
        name="contract",
    )(slots, orbitals, amp0, amp1, right0, right1)


def add_kernel(own0, other0, own1, other1, *outs):
    kept_ref, sent = outs[0], outs[1:]
    half = own0.shape[0] // 2
    for variant, (own, other) in enumerate(((own0, other0), (own1, other1))):
        for n in range(2 * half):
            total = own[n].astype(jnp.float32) + other[n].astype(jnp.float32)
            if n < half:
                kept_ref[variant, n] = total
            elif len(sent) == 2:
                sent[variant][n - half] = total.astype(jnp.bfloat16)
            else:
                sent[0][variant * half + n - half] = total.astype(jnp.bfloat16)


def add_halves(owns, others, count, joined):
    group, half, width = owns[0][0].shape[-3:]
    tile = 2
    flat = [pair for pairs in zip(owns, others) for pair in pairs]
    arrays = [
        array.reshape((-1, group, half, width)) for array, _ in flat
    ]
    sent = [(count, group)] if joined else [(count // 2, group)] * 2
    return pl.pallas_call(
        add_kernel,
        grid=(group // tile,),
        in_specs=[
            pl.BlockSpec((count, tile, half, width), lambda g, at=at: (at, g, 0, 0))
            for _, at in flat
        ],
        out_specs=[pl.BlockSpec((2, count // 2, tile, half, width), lambda g: (0, 0, g, 0, 0))]
        + [pl.BlockSpec((n, tile, half, width), lambda g: (0, g, 0, 0)) for n, _ in sent],
        out_shape=[jax.ShapeDtypeStruct((2, count // 2, group, half, width), jnp.float32)]
        + [jax.ShapeDtypeStruct((n, m, half, width), jnp.bfloat16) for n, m in sent],
        cost_estimate=pl.CostEstimate(
            flops=2 * count * group * half * width,
            bytes_accessed=14 * count * group * half * width,
            transcendentals=0,
        ),
        name="add_halves",
    )(*arrays)


def finish_kernel(core_ref, kept_low, low, kept_high, high0, high1, keep_ref, send_ref):
    core = core_ref[0]
    blocks = PER_OWNER // 2
    highs = (high0, high1)

    def write(order):
        for variant, out_ref in enumerate((keep_ref, send_ref) if order == 0 else (send_ref, keep_ref)):
            for block in range(blocks):
                rows = slice(block * BLOCK, (block + 1) * BLOCK)
                for occ in range(SPLIT):
                    row = block * SPLIT + occ
                    total = kept_low[variant, 0, row] + low[variant, row].astype(jnp.float32)
                    out_ref[occ, rows, :] = total.T
                    total = kept_high[variant, 0, row] + highs[variant][0, row].astype(jnp.float32)
                    out_ref[SPLIT + occ, rows, :] = total.T

    @pl.when(core == 0)
    def _():
        write(0)

    @pl.when(core != 0)
    def _():
        write(1)


def finish(core, kept_low, low, kept_high, high0, high1):
    half, width = low.shape[-2:]
    vmem = pl.BlockSpec(memory_space=pltpu.VMEM)
    shape = jax.ShapeDtypeStruct((2 * SPLIT, PER_OWNER // 2 * width, half), jnp.float32)
    return pl.pallas_call(
        finish_kernel,
        in_specs=[pl.BlockSpec(memory_space=pltpu.SMEM)] + [vmem] * 5,
        out_specs=[vmem, vmem],
        out_shape=[shape, shape],
        cost_estimate=pl.CostEstimate(
            flops=4 * shape.size, bytes_accessed=20 * shape.size, transcendentals=0
        ),
        name="finish",
    )(core, kept_low, low, kept_high, high0, high1)


def join_kernel(core_ref, own_ref, got_ref, out_ref):
    half = own_ref.shape[2]
    core = core_ref[0]

    def write(order):
        for occ in range(own_ref.shape[0]):
            for side, ref in enumerate((own_ref, got_ref) if order == 0 else (got_ref, own_ref)):
                out_ref[:, occ, side * half : (side + 1) * half] = ref[occ]

    @pl.when(core == 0)
    def _():
        write(0)

    @pl.when(core != 0)
    def _():
        write(1)


def join(core, own, got):
    orbitals, rows, half = own.shape
    tile = 64
    return pl.pallas_call(
        join_kernel,
        grid=(rows // tile,),
        in_specs=[pl.BlockSpec(memory_space=pltpu.SMEM)]
        + [pl.BlockSpec((orbitals, tile, half), lambda r: (0, r, 0))] * 2,
        out_specs=pl.BlockSpec((tile, orbitals, 2 * half), lambda r: (r, 0, 0)),
        out_shape=jax.ShapeDtypeStruct((rows, orbitals, 2 * half), jnp.float32),
        cost_estimate=pl.CostEstimate(
            flops=0, bytes_accessed=16 * own.size, transcendentals=0
        ),
        name="join",
    )(core, own, got)


def step_y(value, bits):
    return lax.ppermute(value, "vb", [(j, j ^ bits) for j in range(8)])


def swap_z(value):
    return step_y(value, 4)


def shards(left_fit, right_fit, occ_energy, virt_energy, pair_list, domain_blocks):
    pairs, rows, _ = left_fit.shape
    dom_blocks = domain_blocks.shape[1]
    core = lax.axis_index("pair")
    ea = lax.dynamic_slice_in_dim(virt_energy, lax.axis_index("va") * rows, rows)
    eb = lax.dynamic_slice_in_dim(virt_energy, lax.axis_index("vb") * rows, rows)
    swap = [(0, 1), (1, 0)]
    vb = lax.axis_index("vb")
    table = jnp.concatenate([domain_blocks, pair_list[:, :1]], axis=1)
    both = jnp.stack([table, lax.ppermute(table, "pair", swap)])
    blocks, orbitals = both[:, :, :dom_blocks], both[:, :, dom_blocks]
    apart = (blocks // PER_OWNER) ^ vb
    apart_z, apart_y = apart // 4, apart % 4
    variant = blocks % PER_OWNER // 2
    near = jnp.where(variant == 0, 3, 1)
    code = jnp.where(
        apart_y == 0, 0, jnp.where(apart_y == near, 1, jnp.where(apart_y == 2, 3, 2))
    )
    inner = blocks % 2
    slots_high = (((apart_z * 2 + variant) * 4 + code) * 2 + inner) * SPLIT
    slots_low = (((variant * 4 + code) * 2 + apart_z) * 2 + inner) * SPLIT
    other_right = lax.ppermute(right_fit, "pair", swap)
    count = pairs // CHUNKS
    tiles = coulomb(left_fit, right_fit, 0, count, 1)
    tiles += coulomb(left_fit, right_fit, count, count, CHUNKS - 1, tuple(tiles))
    mirrors = []
    for piece, tile in enumerate(tiles):
        out, back = detour_pairs(piece)
        mid = lax.ppermute(tile, AXES, out)
        mirrors.append(lax.ppermute(mid, AXES, back))
    me = core.reshape(1).astype(jnp.int32)
    ready = (slots_high, slots_low, orbitals)
    keep, send = amplitude(me, occ_energy, pair_list, ea, eb, tiles, mirrors, ready)
    other_amp = lax.ppermute(send, "pair", swap)
    operands = (orbitals, keep, other_amp, right_fit, other_right)
    stay0, stay1, cross = contract(slots_high, *operands, SPLIT, (4, 4, 8))
    crossed = swap_z(cross)
    low0, sent0, low1, sent1 = contract(slots_low, *operands, 0, (4, 4, 4, 4))
    got0, got1 = step_y(sent0, 1), step_y(sent1, 3)
    kept_low, sent0, sent1 = add_halves(
        [(low0, 0), (low1, 0)], [(got0, 0), (got1, 0)], 4, False
    )
    got0, got1 = step_y(sent0, 3), step_y(sent1, 1)
    kept_high, high0, high1 = add_halves(
        [(stay0, 0), (stay1, 0)], [(crossed, 0), (crossed, 1)], 4, False
    )
    more0, more1 = step_y(high0, 1), step_y(high1, 3)
    kept_low, far = add_halves(
        [(kept_low, 0), (kept_low, 1)], [(got0, 0), (got1, 0)], 2, True
    )
    far = swap_z(far)
    kept_high, high0, high1 = add_halves(
        [(kept_high, 0), (kept_high, 1)], [(more0, 0), (more1, 0)], 2, False
    )
    high0, high1 = step_y(high0, 3), step_y(high1, 1)
    own, send = finish(me, kept_low, far, kept_high, high0, high1)
    return join(me, own, lax.ppermute(send, "pair", swap))


def solution(mesh):
    return jax.shard_map(
        shards,
        mesh=mesh,
        in_specs=(
            P("pair", "va", None),
            P("pair", "vb", None),
            P(),
            P(),
            P("pair", None),
            P("pair", None),
        ),
        out_specs=P(("vb", "pair"), None, "va"),
        check_vma=False,
    )
```

```python
import itertools

import jax
import jax.numpy as jnp
from jax import lax
from jax.experimental import pallas as pl
from jax.experimental.pallas import tpu as pltpu
from jax.sharding import PartitionSpec as P


BLOCK = 128
AUX_BLK = 32
CHUNKS = 3
HALVES = 2
SPLIT = 4
PER_OWNER = 4
AXES = ("va", "vb", "pair")
DETOURS = (
    ((0, 0, 1), (0, 1, 2), (2, 3, 3), (2, 1, 0), (0, 3, 2), (1, 3, 0)),
    ((0, 0, 1), (3, 3, 1), (1, 0, 0), (2, 3, 0), (0, 1, 3), (0, 1, 0)),
)


def to_flat(x, y, z, core):
    va = x * 2 + z // 2
    vb = (z % 2) * 4 + y
    return (va * 8 + vb) * 2 + core


def mirror_chip(x, y, z):
    va, vb = x * 2 + z // 2, (z % 2) * 4 + y
    va, vb = vb, va
    return va // 2, vb % 4, (va % 2) * 2 + vb // 4


def detour_pairs(part, piece):
    out, back = [], []
    for x, y, z, core in itertools.product(range(4), range(4), range(4), range(2)):
        dx, dy, dz = DETOURS[part][core * CHUNKS + piece]
        mid = ((x + dx) % 4, (y + dy) % 4, (z + dz) % 4)
        out.append((to_flat(x, y, z, core), to_flat(*mid, core)))
        back.append((to_flat(*mid, core), to_flat(*mirror_chip(x, y, z), core)))
    return out, back


def coulomb_kernel(start, chunks, left_ref, right_ref, *refs):
    per = 1 + HALVES
    out_refs, (left_buf, right_buf, sems) = refs[-3 - per * chunks : -3], refs[-3:]
    count, rows, _ = out_refs[0].shape
    width = rows // HALVES
    copies = []
    for p in range(count * chunks):
        pair = [
            pltpu.make_async_copy(left_ref.at[start + p], left_buf.at[p], sems.at[0, p]),
            pltpu.make_async_copy(right_ref.at[start + p], right_buf.at[p], sems.at[1, p]),
        ]
        for copy in pair:
            copy.start()
        copies.append(pair)
    for p, pair in enumerate(copies):
        for copy in pair:
            copy.wait()
        tile = lax.dot_general(
            left_buf[p], right_buf[p], (((1,), (1,)), ((), ())), preferred_element_type=jnp.float32
        ).astype(jnp.bfloat16)
        outs = out_refs[p // count * per : (p // count + 1) * per]
        outs[0][p % count] = tile
        for part in range(HALVES):
            outs[1 + part][p % count] = tile[:, part * width : (part + 1) * width]


def coulomb(left_fit, right_fit, start, count, chunks, after=()):
    _, rows, dom = left_fit.shape
    total = count * chunks
    hbm = pl.BlockSpec(memory_space=pl.ANY)
    shapes = [jax.ShapeDtypeStruct((count, rows, rows), jnp.bfloat16)]
    shapes += [jax.ShapeDtypeStruct((count, rows, rows // HALVES), jnp.bfloat16)] * HALVES
    out = pl.pallas_call(
        lambda *refs: coulomb_kernel(start, chunks, *refs),
        in_specs=[hbm] * (2 + len(after)),
        out_specs=[pl.BlockSpec(memory_space=pltpu.VMEM)] * (len(shapes) * chunks),
        out_shape=shapes * chunks,
        scratch_shapes=[
            pltpu.VMEM((total, rows, dom), jnp.bfloat16),
            pltpu.VMEM((total, rows, dom), jnp.bfloat16),
            pltpu.SemaphoreType.DMA((2, total)),
        ],
        cost_estimate=pl.CostEstimate(
            flops=2 * total * rows * rows * dom,
            bytes_accessed=4 * total * rows * dom + 4 * total * rows * rows,
            transcendentals=0,
        ),
        compiler_params=pltpu.CompilerParams(vmem_limit_bytes=60 << 20),
        name="coulomb",
    )(left_fit, right_fit, *after)
    return [out[c * len(shapes) : (c + 1) * len(shapes)] for c in range(chunks)]


def gate(values, after):
    hbm = pl.BlockSpec(memory_space=pl.ANY)
    count = len(values)
    return pl.pallas_call(
        lambda *refs: None,
        in_specs=[hbm] * (count + len(after)),
        out_specs=[hbm] * count,
        out_shape=[jax.ShapeDtypeStruct(value.shape, value.dtype) for value in values],
        input_output_aliases={n: n for n in range(count)},
        name="gate",
    )(*values, *after)


def amplitude_kernel(part, chunks, *refs):
    core_ref, occ_ref, pair_ref = refs[:3]
    keep_ref, send_ref, work_ref = refs[-3:]
    ea_ref, eb_ref = refs[-5 - 2 * chunks : -3 - 2 * chunks]
    tiles = refs[-3 - 2 * chunks : -3 - chunks]
    mirrors = refs[-3 - chunks : -3]
    share = keep_ref.shape[1]
    count, _, width = mirrors[0].shape
    core = core_ref[0]
    rows = slice(part * width, (part + 1) * width)
    base = ea_ref[rows, :] + eb_ref[...]
    mine = pl.multiple_of(core * share, share)
    other = pl.multiple_of((1 - core) * share, share)
    for chunk in range(chunks):
        for row in range(count):
            p = chunk * count + row
            gap = base - occ_ref[pair_ref[p, 0]] - occ_ref[pair_ref[p, 1]]
            tile = tiles[chunk][row, rows, :].astype(jnp.float32)
            swapped = mirrors[chunk][row].astype(jnp.float32).T
            work_ref[p % 2] = ((2.0 * tile - swapped) / gap).astype(jnp.bfloat16)
            keep_ref[p] = work_ref[p % 2, pl.ds(mine, share), :]
            send_ref[p] = work_ref[p % 2, pl.ds(other, share), :]


def amplitude(part, core, occ_energy, pair_list, ea, eb, tiles, mirrors, ready):
    pairs = pair_list.shape[0]
    _, rows, width = mirrors[0].shape
    smem = pl.BlockSpec(memory_space=pltpu.SMEM)
    vmem = pl.BlockSpec(memory_space=pltpu.VMEM)
    chunks = len(tiles)
    shape = jax.ShapeDtypeStruct((pairs, width // 2, rows), jnp.bfloat16)
    return pl.pallas_call(
        lambda *refs: amplitude_kernel(part, chunks, *refs),
        in_specs=[smem] * (3 + len(ready)) + [vmem] * (2 + 2 * chunks),
        out_specs=[vmem, vmem],
        out_shape=[shape, shape],
        scratch_shapes=[pltpu.VMEM((2, width, rows), jnp.bfloat16)],
        cost_estimate=pl.CostEstimate(
            flops=10 * pairs * rows * width,
            bytes_accessed=6 * pairs * rows * width,
            transcendentals=0,
        ),
        name="amplitude",
    )(
        core, occ_energy, pair_list, *ready, ea.reshape(rows, 1), eb.reshape(1, rows), *tiles, *mirrors
    )


def contract_kernel(low, slot_ref, occ_ref, amp0, amp1, right0, right1, *refs):
    out_refs, (buf_ref, acc_ref, stage_ref, in_sems, out_sems) = refs[:-5], refs[-5:]
    pairs = amp0.shape[0]
    dom_blocks = slot_ref.shape[2]
    sides = ((amp0, right0), (amp1, right1))

    def taken(side, p):
        return (occ_ref[side, p] >= low) & (occ_ref[side, p] < low + SPLIT)

    def load(side, p):
        return pltpu.make_async_copy(
            sides[side][1].at[p], buf_ref.at[side, p], in_sems.at[side, p]
        )

    for side in range(2):

        @pl.loop(0, pairs)
        def _(p):
            @pl.when(taken(side, p))
            def _():
                load(side, p).start()

    acc_ref[...] = jnp.zeros_like(acc_ref)
    for side in range(2):

        @pl.loop(0, pairs)
        def _(p):
            @pl.when(taken(side, p))
            def _():
                load(side, p).wait()
                part = jnp.dot(sides[side][0][p], buf_ref[side, p], preferred_element_type=jnp.float32)
                for k in range(dom_blocks):
                    slot = slot_ref[side, p, k] + occ_ref[side, p] - low
                    acc_ref[slot] += part[:, k * BLOCK : (k + 1) * BLOCK]

    group = out_refs[0].shape[1]
    copies = []
    for out_ref in out_refs:
        for block in range(out_ref.shape[0]):
            place = len(copies)
            stage_ref[place] = acc_ref[place * group : (place + 1) * group].astype(stage_ref.dtype)
            copy = pltpu.make_async_copy(
                stage_ref.at[place], out_ref.at[block], out_sems.at[place]
            )
            copy.start()
            copies.append(copy)
    for copy in copies:
        copy.wait()


def contract(slots, orbitals, amp0, amp1, right0, right1, low, outs):
    pairs, half, rows = amp0.shape
    dom = right0.shape[2]
    total = AUX_BLK * SPLIT
    places = sum(outs)
    group = total // places
    smem = pl.BlockSpec(memory_space=pltpu.SMEM)
    vmem = pl.BlockSpec(memory_space=pltpu.VMEM)
    hbm = pl.BlockSpec(memory_space=pl.ANY)
    return pl.pallas_call(
        lambda *refs: contract_kernel(low, *refs),
        in_specs=[smem, smem, vmem, vmem, hbm, hbm],
        out_specs=[hbm] * len(outs),
        out_shape=[jax.ShapeDtypeStruct((n, group, half, BLOCK), jnp.bfloat16) for n in outs],
        scratch_shapes=[
            pltpu.VMEM((2, pairs, rows, dom), jnp.bfloat16),
            pltpu.VMEM((total, half, BLOCK), jnp.float32),
            pltpu.VMEM((places, group, half, BLOCK), jnp.bfloat16),
            pltpu.SemaphoreType.DMA((2, pairs)),
            pltpu.SemaphoreType.DMA((places,)),
        ],
        cost_estimate=pl.CostEstimate(
            flops=2 * pairs * half * rows * dom,
            bytes_accessed=2 * pairs * rows * dom + 2 * total * half * BLOCK,
            transcendentals=0,
        ),
        compiler_params=pltpu.CompilerParams(vmem_limit_bytes=60 << 20),
        name="contract",
    )(slots, orbitals, amp0, amp1, right0, right1)


def add_kernel(own0, other0, own1, other1, *outs):
    kept_ref, sent = outs[0], outs[1:]
    half = own0.shape[0] // 2
    for variant, (own, other) in enumerate(((own0, other0), (own1, other1))):
        for n in range(2 * half):
            total = own[n].astype(jnp.float32) + other[n].astype(jnp.float32)
            if n < half:
                kept_ref[variant, n] = total
            elif len(sent) == 2:
                sent[variant][n - half] = total.astype(jnp.bfloat16)
            else:
                sent[0][variant * half + n - half] = total.astype(jnp.bfloat16)


def add_halves(owns, others, count, joined):
    group, half, width = owns[0][0].shape[-3:]
    tile = 2
    flat = [pair for pairs in zip(owns, others) for pair in pairs]
    arrays = [
        array.reshape((-1, group, half, width)) for array, _ in flat
    ]
    sent = [(count, group)] if joined else [(count // 2, group)] * 2
    return pl.pallas_call(
        add_kernel,
        grid=(group // tile,),
        in_specs=[
            pl.BlockSpec((count, tile, half, width), lambda g, at=at: (at, g, 0, 0))
            for _, at in flat
        ],
        out_specs=[pl.BlockSpec((2, count // 2, tile, half, width), lambda g: (0, 0, g, 0, 0))]
        + [pl.BlockSpec((n, tile, half, width), lambda g: (0, g, 0, 0)) for n, _ in sent],
        out_shape=[jax.ShapeDtypeStruct((2, count // 2, group, half, width), jnp.float32)]
        + [jax.ShapeDtypeStruct((n, m, half, width), jnp.bfloat16) for n, m in sent],
        cost_estimate=pl.CostEstimate(
            flops=2 * count * group * half * width,
            bytes_accessed=14 * count * group * half * width,
            transcendentals=0,
        ),
        name="add_halves",
    )(*arrays)


def finish_kernel(core_ref, *refs):
    ins, (keep_ref, send_ref) = refs[:-2], refs[-2:]
    core = core_ref[0]
    blocks = PER_OWNER // 2
    halves = [ins[5 * part : 5 * part + 5] for part in range(HALVES)]

    def low_sum(variant, row):
        return jnp.concatenate(
            [kept[variant, 0, row] + far[variant, row].astype(jnp.float32) for kept, far, *_ in halves],
            axis=0,
        )

    def high_sum(variant, row):
        return jnp.concatenate(
            [
                kept[variant, 0, row] + (high0, high1)[variant][0, row].astype(jnp.float32)
                for _, _, kept, high0, high1 in halves
            ],
            axis=0,
        )

    def write(order):
        for variant, out_ref in enumerate((keep_ref, send_ref) if order == 0 else (send_ref, keep_ref)):
            for block in range(blocks):
                rows = slice(block * BLOCK, (block + 1) * BLOCK)
                for occ in range(SPLIT):
                    row = block * SPLIT + occ
                    out_ref[occ, rows, :] = low_sum(variant, row).T
                    out_ref[SPLIT + occ, rows, :] = high_sum(variant, row).T

    @pl.when(core == 0)
    def _():
        write(0)

    @pl.when(core != 0)
    def _():
        write(1)


def finish(core, parts):
    share, width = parts[0][0].shape[-2:]
    vmem = pl.BlockSpec(memory_space=pltpu.VMEM)
    shape = jax.ShapeDtypeStruct(
        (2 * SPLIT, PER_OWNER // 2 * width, HALVES * share), jnp.float32
    )
    return pl.pallas_call(
        finish_kernel,
        in_specs=[pl.BlockSpec(memory_space=pltpu.SMEM)] + [vmem] * (5 * len(parts)),
        out_specs=[vmem, vmem],
        out_shape=[shape, shape],
        cost_estimate=pl.CostEstimate(
            flops=4 * shape.size, bytes_accessed=20 * shape.size, transcendentals=0
        ),
        name="finish",
    )(core, *[array for part in parts for array in part])


def join_kernel(core_ref, own_ref, got_ref, out_ref):
    width = own_ref.shape[2]
    core = core_ref[0]
    left = lax.broadcasted_iota(jnp.int32, own_ref.shape[1:], 1) < width // 2

    def write(order):
        first, second = (own_ref, got_ref) if order == 0 else (got_ref, own_ref)
        for occ in range(own_ref.shape[0]):
            low, high = first[occ], second[occ]
            out_ref[:, occ, :width] = jnp.where(left, low, pltpu.roll(high, width // 2, 1))
            out_ref[:, occ, width:] = jnp.where(left, pltpu.roll(low, width // 2, 1), high)

    @pl.when(core == 0)
    def _():
        write(0)

    @pl.when(core != 0)
    def _():
        write(1)


def join(core, own, got):
    orbitals, rows, width = own.shape
    tile = 64
    return pl.pallas_call(
        join_kernel,
        grid=(rows // tile,),
        in_specs=[pl.BlockSpec(memory_space=pltpu.SMEM)]
        + [pl.BlockSpec((orbitals, tile, width), lambda r: (0, r, 0))] * 2,
        out_specs=pl.BlockSpec((tile, orbitals, 2 * width), lambda r: (r, 0, 0)),
        out_shape=jax.ShapeDtypeStruct((rows, orbitals, 2 * width), jnp.float32),
        cost_estimate=pl.CostEstimate(
            flops=0, bytes_accessed=16 * own.size, transcendentals=0
        ),
        name="join",
    )(core, own, got)


def step_y(value, bits):
    return lax.ppermute(value, "vb", [(j, j ^ bits) for j in range(8)])


def swap_z(value):
    return step_y(value, 4)


def reduce_half(slots_high, slots_low, operands):
    stay0, stay1, cross = contract(slots_high, *operands, SPLIT, (4, 4, 8))
    crossed = swap_z(cross)
    low0, sent0, low1, sent1 = contract(slots_low, *operands, 0, (4, 4, 4, 4))
    got0, got1 = step_y(sent0, 1), step_y(sent1, 3)
    kept_low, sent0, sent1 = add_halves([(low0, 0), (low1, 0)], [(got0, 0), (got1, 0)], 4, False)
    got0, got1 = step_y(sent0, 3), step_y(sent1, 1)
    kept_high, high0, high1 = add_halves(
        [(stay0, 0), (stay1, 0)], [(crossed, 0), (crossed, 1)], 4, False
    )
    more0, more1 = step_y(high0, 1), step_y(high1, 3)
    kept_low, far = add_halves(
        [(kept_low, 0), (kept_low, 1)], [(got0, 0), (got1, 0)], 2, True
    )
    far = swap_z(far)
    kept_high, high0, high1 = add_halves(
        [(kept_high, 0), (kept_high, 1)], [(more0, 0), (more1, 0)], 2, False
    )
    return (kept_low, far, kept_high, step_y(high0, 3), step_y(high1, 1)), (low0, stay0)


def program(left_fit, right_fit, occ_energy, virt_energy, pair_list, domain_blocks):
    pairs, rows, _ = left_fit.shape
    dom_blocks = domain_blocks.shape[1]
    core = lax.axis_index("pair")
    ea = lax.dynamic_slice_in_dim(virt_energy, lax.axis_index("va") * rows, rows)
    eb = lax.dynamic_slice_in_dim(virt_energy, lax.axis_index("vb") * rows, rows)
    swap = [(0, 1), (1, 0)]
    vb = lax.axis_index("vb")
    table = jnp.concatenate([domain_blocks, pair_list[:, :1]], axis=1)
    both = jnp.stack([table, lax.ppermute(table, "pair", swap)])
    blocks, orbitals = both[:, :, :dom_blocks], both[:, :, dom_blocks]
    apart = (blocks // PER_OWNER) ^ vb
    apart_z, apart_y = apart // 4, apart % 4
    variant = blocks % PER_OWNER // 2
    near = jnp.where(variant == 0, 3, 1)
    code = jnp.where(
        apart_y == 0, 0, jnp.where(apart_y == near, 1, jnp.where(apart_y == 2, 3, 2))
    )
    inner = blocks % 2
    slots_high = (((apart_z * 2 + variant) * 4 + code) * 2 + inner) * SPLIT
    slots_low = (((variant * 4 + code) * 2 + apart_z) * 2 + inner) * SPLIT
    other_right = lax.ppermute(right_fit, "pair", swap)
    count = pairs // CHUNKS
    made = coulomb(left_fit, right_fit, 0, count, 1)
    made += coulomb(left_fit, right_fit, count, count, CHUNKS - 1, made[0][:1])
    me = core.reshape(1).astype(jnp.int32)
    tiles = [arrays[0] for arrays in made]
    ready = (slots_high, slots_low, orbitals)
    mirrors, parts, mids = [], [], []
    for part in range(HALVES):
        values = [arrays[1 + part] for arrays in made]
        routes = [detour_pairs(part, piece) for piece in range(CHUNKS)]
        if part:
            values = gate(values, mids)
        mids = [lax.ppermute(value, AXES, out) for value, (out, _) in zip(values, routes)]
        values = gate(mids, mirrors[-1]) if part else mids
        mirrors.append([lax.ppermute(mid, AXES, back) for mid, (_, back) in zip(values, routes)])
    for part in range(HALVES):
        arrived = mirrors[part]
        if part:
            arrived = gate(arrived, parts[-1][1])
        keep, send = amplitude(part, me, occ_energy, pair_list, ea, eb, tiles, arrived, ready)
        other_amp = lax.ppermute(send, "pair", swap)
        operands = (orbitals, keep, other_amp, right_fit, other_right)
        parts.append(reduce_half(slots_high, slots_low, operands))
    parts = [part[0] for part in parts]
    own, send = finish(me, parts)
    return join(me, own, lax.ppermute(send, "pair", swap))


def solution(mesh):
    return jax.shard_map(
        program,
        mesh=mesh,
        in_specs=(
            P("pair", "va", None),
            P("pair", "vb", None),
            P(),
            P(),
            P("pair", None),
            P("pair", None),
        ),
        out_specs=P(("vb", "pair"), None, "va"),
        check_vma=False,
    )
```

```python
import itertools

import jax
import jax.numpy as jnp
from jax import lax
from jax.experimental import pallas as pl
from jax.experimental.pallas import tpu as pltpu
from jax.sharding import PartitionSpec as P


BLOCK = 128
AUX_BLK = 32
CHUNKS = 5
SPLIT = 4
PER_OWNER = 4
AXES = ("va", "vb", "pair")
DETOURS = (
    (1, 0, 3), (0, 2, 0), (1, 0, 0), (2, 1, 0), (2, 2, 2),
    (3, 0, 2), (0, 3, 1), (3, 3, 1), (1, 1, 1), (3, 1, 3),
)


def to_flat(x, y, z, core):
    va = x * 2 + z // 2
    vb = (z % 2) * 4 + y
    return (va * 8 + vb) * 2 + core


def mirror_chip(x, y, z):
    va, vb = x * 2 + z // 2, (z % 2) * 4 + y
    va, vb = vb, va
    return va // 2, vb % 4, (va % 2) * 2 + vb // 4


def detour_pairs(piece):
    out, back = [], []
    for x, y, z, core in itertools.product(range(4), range(4), range(4), range(2)):
        dx, dy, dz = DETOURS[core * CHUNKS + piece]
        mid = ((x + dx) % 4, (y + dy) % 4, (z + dz) % 4)
        out.append((to_flat(x, y, z, core), to_flat(*mid, core)))
        back.append((to_flat(*mid, core), to_flat(*mirror_chip(x, y, z), core)))
    return out, back


def coulomb_kernel(start, chunks, left_ref, right_ref, *refs):
    out_refs, (left_buf, right_buf, sems) = refs[-3 - chunks : -3], refs[-3:]
    count = out_refs[0].shape[0]
    copies = []
    for p in range(count * len(out_refs)):
        pair = [
            pltpu.make_async_copy(left_ref.at[start + p], left_buf.at[p], sems.at[0, p]),
            pltpu.make_async_copy(right_ref.at[start + p], right_buf.at[p], sems.at[1, p]),
        ]
        for copy in pair:
            copy.start()
        copies.append(pair)
    for p, pair in enumerate(copies):
        for copy in pair:
            copy.wait()
        out_refs[p // count][p % count] = lax.dot_general(
            left_buf[p], right_buf[p], (((1,), (1,)), ((), ())), preferred_element_type=jnp.float32
        ).astype(jnp.bfloat16)


def coulomb(left_fit, right_fit, start, count, chunks, after=()):
    _, rows, dom = left_fit.shape
    total = count * chunks
    hbm = pl.BlockSpec(memory_space=pl.ANY)
    return pl.pallas_call(
        lambda *refs: coulomb_kernel(start, chunks, *refs),
        in_specs=[hbm] * (2 + len(after)),
        out_specs=[pl.BlockSpec(memory_space=pltpu.VMEM)] * chunks,
        out_shape=[jax.ShapeDtypeStruct((count, rows, rows), jnp.bfloat16)] * chunks,
        scratch_shapes=[
            pltpu.VMEM((total, rows, dom), jnp.bfloat16),
            pltpu.VMEM((total, rows, dom), jnp.bfloat16),
            pltpu.SemaphoreType.DMA((2, total)),
        ],
        cost_estimate=pl.CostEstimate(
            flops=2 * total * rows * rows * dom,
            bytes_accessed=4 * total * rows * dom + 2 * total * rows * rows,
            transcendentals=0,
        ),
        compiler_params=pltpu.CompilerParams(vmem_limit_bytes=60 << 20),
        name="coulomb",
    )(left_fit, right_fit, *after)


def fetch(refs, buf_ref, sems):
    copies = [
        pltpu.make_async_copy(ref, buf_ref.at[n], sems.at[n]) for n, ref in enumerate(refs)
    ]
    for copy in copies:
        copy.start()
    return copies


def amplitude_kernel(chunks, *refs):
    core_ref, occ_ref, pair_ref = refs[:3]
    keep_ref, send_ref, work_ref, buf_ref, sems = refs[-5:]
    refs = refs[:-5]
    ea_ref, eb_ref = refs[-2 - 2 * chunks : -2 * chunks]
    copies = fetch(refs[-2 * chunks :], buf_ref, sems)
    tiles = [buf_ref.at[n] for n in range(chunks)]
    mirrors = [buf_ref.at[chunks + n] for n in range(chunks)]
    half = keep_ref.shape[1]
    count = tiles[0].shape[0]
    core = core_ref[0]
    base = ea_ref[...] + eb_ref[...]
    mine = pl.multiple_of(core * half, half)
    other = pl.multiple_of((1 - core) * half, half)
    for chunk in range(chunks):
        copies[chunk].wait()
        copies[chunks + chunk].wait()
        for row in range(count):
            p = chunk * count + row
            gap = base - occ_ref[pair_ref[p, 0]] - occ_ref[pair_ref[p, 1]]
            tile = tiles[chunk][row].astype(jnp.float32)
            swapped = mirrors[chunk][row].astype(jnp.float32).T
            work_ref[p % 2] = ((2.0 * tile - swapped) / gap).astype(jnp.bfloat16)
            keep_ref[p] = work_ref[p % 2, pl.ds(mine, half), :]
            send_ref[p] = work_ref[p % 2, pl.ds(other, half), :]


def amplitude(core, occ_energy, pair_list, ea, eb, tiles, mirrors, ready):
    pairs = pair_list.shape[0]
    rows = tiles[0].shape[1]
    smem = pl.BlockSpec(memory_space=pltpu.SMEM)
    vmem = pl.BlockSpec(memory_space=pltpu.VMEM)
    hbm = pl.BlockSpec(memory_space=pl.ANY)
    chunks = len(tiles)
    shape = jax.ShapeDtypeStruct((pairs, rows // 2, rows), jnp.bfloat16)
    return pl.pallas_call(
        lambda *refs: amplitude_kernel(chunks, *refs),
        in_specs=[smem] * (3 + len(ready)) + [vmem] * 2 + [hbm] * (2 * chunks),
        out_specs=[vmem, vmem],
        out_shape=[shape, shape],
        scratch_shapes=[
            pltpu.VMEM((2, rows, rows), jnp.bfloat16),
            pltpu.VMEM((2 * chunks,) + tiles[0].shape, jnp.bfloat16),
            pltpu.SemaphoreType.DMA((2 * chunks,)),
        ],
        cost_estimate=pl.CostEstimate(
            flops=10 * pairs * rows * rows, bytes_accessed=6 * pairs * rows * rows, transcendentals=0
        ),
        name="amplitude",
    )(
        core, occ_energy, pair_list, *ready, ea.reshape(rows, 1), eb.reshape(1, rows), *tiles, *mirrors
    )


def contract_kernel(low, slot_ref, occ_ref, amp0, amp1, right0, right1, *refs):
    out_refs, (amp_ref, amp_sems, buf_ref, acc_ref, stage_ref, in_sems, out_sems) = refs[:-7], refs[-7:]
    pairs = amp0.shape[0]
    amps = fetch((amp0, amp1), amp_ref, amp_sems)
    dom_blocks = slot_ref.shape[2]
    sides = ((amp0, right0), (amp1, right1))

    def taken(side, p):
        return (occ_ref[side, p] >= low) & (occ_ref[side, p] < low + SPLIT)

    def load(side, p):
        return pltpu.make_async_copy(
            sides[side][1].at[p], buf_ref.at[side, p], in_sems.at[side, p]
        )

    for side in range(2):

        @pl.loop(0, pairs)
        def _(p):
            @pl.when(taken(side, p))
            def _():
                load(side, p).start()

    acc_ref[...] = jnp.zeros_like(acc_ref)
    for side in range(2):
        amps[side].wait()

        @pl.loop(0, pairs)
        def _(p):
            @pl.when(taken(side, p))
            def _():
                load(side, p).wait()
                part = jnp.dot(amp_ref[side, p], buf_ref[side, p], preferred_element_type=jnp.float32)
                for k in range(dom_blocks):
                    slot = slot_ref[side, p, k] + occ_ref[side, p] - low
                    acc_ref[slot] += part[:, k * BLOCK : (k + 1) * BLOCK]

    group = out_refs[0].shape[1]
    copies = []
    for out_ref in out_refs:
        for block in range(out_ref.shape[0]):
            place = len(copies)
            stage_ref[place] = acc_ref[place * group : (place + 1) * group].astype(stage_ref.dtype)
            copy = pltpu.make_async_copy(
                stage_ref.at[place], out_ref.at[block], out_sems.at[place]
            )
            copy.start()
            copies.append(copy)
    for copy in copies:
        copy.wait()


def contract(slots, orbitals, amp0, amp1, right0, right1, low, outs):
    pairs, half, rows = amp0.shape
    dom = right0.shape[2]
    total = AUX_BLK * SPLIT
    places = sum(outs)
    group = total // places
    smem = pl.BlockSpec(memory_space=pltpu.SMEM)
    hbm = pl.BlockSpec(memory_space=pl.ANY)
    return pl.pallas_call(
        lambda *refs: contract_kernel(low, *refs),
        in_specs=[smem, smem, hbm, hbm, hbm, hbm],
        out_specs=[hbm] * len(outs),
        out_shape=[jax.ShapeDtypeStruct((n, group, half, BLOCK), jnp.bfloat16) for n in outs],
        scratch_shapes=[
            pltpu.VMEM((2, pairs, half, rows), jnp.bfloat16),
            pltpu.SemaphoreType.DMA((2,)),
            pltpu.VMEM((2, pairs, rows, dom), jnp.bfloat16),
            pltpu.VMEM((total, half, BLOCK), jnp.float32),
            pltpu.VMEM((places, group, half, BLOCK), jnp.bfloat16),
            pltpu.SemaphoreType.DMA((2, pairs)),
            pltpu.SemaphoreType.DMA((places,)),
        ],
        cost_estimate=pl.CostEstimate(
            flops=2 * pairs * half * rows * dom,
            bytes_accessed=2 * pairs * rows * dom + 2 * total * half * BLOCK,
            transcendentals=0,
        ),
        compiler_params=pltpu.CompilerParams(vmem_limit_bytes=60 << 20),
        name="contract",
    )(slots, orbitals, amp0, amp1, right0, right1)


def add_kernel(places, own0, other0, own1, other1, *refs):
    outs, (own_buf, other_buf, kept_buf, sent_buf, in_sems, out_sems) = refs[:-6], refs[-6:]
    kept_ref, sent = outs[0], outs[1:]
    count = own_buf.shape[1]
    half = count // 2
    order = [(variant, n) for n in [*range(half, count), *range(half)] for variant in range(2)]
    loads = {}
    for variant, n in order:
        own, other = ((own0, other0), (own1, other1))[variant]
        own_at, other_at = places[2 * variant], places[2 * variant + 1]
        loads[variant, n] = [
            pltpu.make_async_copy(
                own.at[own_at * count + n], own_buf.at[variant, n], in_sems.at[0, variant, n]
            ),
            pltpu.make_async_copy(
                other.at[other_at * count + n], other_buf.at[variant, n], in_sems.at[1, variant, n]
            ),
        ]
        for copy in loads[variant, n]:
            copy.start()
    stores = []
    for variant, n in order:
        for copy in loads[variant, n]:
            copy.wait()
        total = own_buf[variant, n].astype(jnp.float32) + other_buf[variant, n].astype(jnp.float32)
        if n < half:
            kept_buf[variant, n] = total
            source, target = kept_buf.at[variant, n], kept_ref.at[variant, n]
        else:
            sent_buf[variant, n - half] = total.astype(jnp.bfloat16)
            source = sent_buf.at[variant, n - half]
            if len(sent) == 2:
                target = sent[variant].at[n - half]
            else:
                target = sent[0].at[variant * half + n - half]
        store = pltpu.make_async_copy(source, target, out_sems.at[variant, n])
        store.start()
        stores.append(store)
    for store in stores:
        store.wait()


def add_halves(owns, others, count, joined):
    group, half, width = owns[0][0].shape[-3:]
    flat = [pair for pairs in zip(owns, others) for pair in pairs]
    arrays = [array.reshape((-1, group, half, width)) for array, _ in flat]
    places = [at for _, at in flat]
    sent = [count] if joined else [count // 2] * 2
    hbm = pl.BlockSpec(memory_space=pl.ANY)
    return pl.pallas_call(
        lambda *refs: add_kernel(places, *refs),
        in_specs=[hbm] * 4,
        out_specs=[hbm] * (1 + len(sent)),
        out_shape=[jax.ShapeDtypeStruct((2, count // 2, group, half, width), jnp.float32)]
        + [jax.ShapeDtypeStruct((n, group, half, width), jnp.bfloat16) for n in sent],
        scratch_shapes=[
            pltpu.VMEM((2, count, group, half, width), arrays[0].dtype),
            pltpu.VMEM((2, count, group, half, width), arrays[1].dtype),
            pltpu.VMEM((2, count // 2, group, half, width), jnp.float32),
            pltpu.VMEM((2, count // 2, group, half, width), jnp.bfloat16),
            pltpu.SemaphoreType.DMA((2, 2, count)),
            pltpu.SemaphoreType.DMA((2, count)),
        ],
        cost_estimate=pl.CostEstimate(
            flops=2 * count * group * half * width,
            bytes_accessed=14 * count * group * half * width,
            transcendentals=0,
        ),
        name="add_halves",
    )(*arrays)


def finish_kernel(core_ref, kept_low_in, low_in, kept_high_in, *refs):
    highs_in, (keep_ref, send_ref, kept_buf, low, highs, sems) = refs[:2], refs[2:]
    core = core_ref[0]
    blocks = PER_OWNER // 2
    copies = [
        pltpu.make_async_copy(source, target, sems.at[n])
        for n, (source, target) in enumerate(
            (
                (kept_low_in, kept_buf.at[0]),
                (low_in, low),
                (kept_high_in, kept_buf.at[1]),
                (highs_in[0], highs.at[0]),
                (highs_in[1], highs.at[1]),
            )
        )
    ]
    for copy in copies:
        copy.start()
    for copy in copies:
        copy.wait()
    kept_low, kept_high = kept_buf.at[0], kept_buf.at[1]

    def write(order):
        for variant, out_ref in enumerate((keep_ref, send_ref) if order == 0 else (send_ref, keep_ref)):
            for block in range(blocks):
                rows = slice(block * BLOCK, (block + 1) * BLOCK)
                for occ in range(SPLIT):
                    row = block * SPLIT + occ
                    total = kept_low[variant, 0, row] + low[variant, row].astype(jnp.float32)
                    out_ref[occ, rows, :] = total.T
                    total = kept_high[variant, 0, row] + highs[variant][0, row].astype(jnp.float32)
                    out_ref[SPLIT + occ, rows, :] = total.T

    @pl.when(core == 0)
    def _():
        write(0)

    @pl.when(core != 0)
    def _():
        write(1)


def finish(core, kept_low, low, kept_high, high0, high1):
    half, width = low.shape[-2:]
    vmem = pl.BlockSpec(memory_space=pltpu.VMEM)
    shape = jax.ShapeDtypeStruct((2 * SPLIT, PER_OWNER // 2 * width, half), jnp.float32)
    return pl.pallas_call(
        finish_kernel,
        in_specs=[pl.BlockSpec(memory_space=pltpu.SMEM)] + [pl.BlockSpec(memory_space=pl.ANY)] * 5,
        out_specs=[vmem, vmem],
        out_shape=[shape, shape],
        scratch_shapes=[
            pltpu.VMEM((2,) + kept_low.shape, jnp.float32),
            pltpu.VMEM(low.shape, low.dtype),
            pltpu.VMEM((2,) + high0.shape, high0.dtype),
            pltpu.SemaphoreType.DMA((5,)),
        ],
        cost_estimate=pl.CostEstimate(
            flops=4 * shape.size, bytes_accessed=20 * shape.size, transcendentals=0
        ),
        name="finish",
    )(core, kept_low, low, kept_high, high0, high1)


def join_kernel(tile, core_ref, own_in, got_in, out_ref, buf_ref, out_buf, in_sems, out_sems):
    orbitals, rows, half = own_in.shape
    core = core_ref[0]
    steps = rows // tile
    loads = []
    for step in range(steps):
        part = slice(step * tile, (step + 1) * tile)
        loads.append(
            [
                pltpu.make_async_copy(
                    source.at[:, part, :], buf_ref.at[n, :, part, :], in_sems.at[n, step]
                )
                for n, source in enumerate((own_in, got_in))
            ]
        )
        for copy in loads[-1]:
            copy.start()
    stores = []
    for step in range(steps):
        part = slice(step * tile, (step + 1) * tile)
        for copy in loads[step]:
            copy.wait()

        def write(order):
            for occ in range(orbitals):
                for side in range(2):
                    out_buf[part, occ, side * half : (side + 1) * half] = buf_ref[
                        side if order == 0 else 1 - side, occ, part, :
                    ]

        @pl.when(core == 0)
        def _():
            write(0)

        @pl.when(core != 0)
        def _():
            write(1)

        store = pltpu.make_async_copy(out_buf.at[part], out_ref.at[part], out_sems.at[step])
        store.start()
        stores.append(store)
    for store in stores:
        store.wait()


def join(core, own, got):
    orbitals, rows, half = own.shape
    tile = 64
    hbm = pl.BlockSpec(memory_space=pl.ANY)
    shape = jax.ShapeDtypeStruct((rows, orbitals, 2 * half), jnp.float32)
    return pl.pallas_call(
        lambda *refs: join_kernel(tile, *refs),
        in_specs=[pl.BlockSpec(memory_space=pltpu.SMEM), hbm, hbm],
        out_specs=hbm,
        out_shape=shape,
        scratch_shapes=[
            pltpu.VMEM((2,) + own.shape, jnp.float32),
            pltpu.VMEM(shape.shape, jnp.float32),
            pltpu.SemaphoreType.DMA((2, rows // tile)),
            pltpu.SemaphoreType.DMA((rows // tile,)),
        ],
        cost_estimate=pl.CostEstimate(
            flops=0, bytes_accessed=16 * own.size, transcendentals=0
        ),
        name="join",
    )(core, own, got)


def step_y(value, bits):
    return lax.ppermute(value, "vb", [(j, j ^ bits) for j in range(8)])


def swap_z(value):
    return step_y(value, 4)


def program(left_fit, right_fit, occ_energy, virt_energy, pair_list, domain_blocks):
    pairs, rows, _ = left_fit.shape
    dom_blocks = domain_blocks.shape[1]
    core = lax.axis_index("pair")
    ea = lax.dynamic_slice_in_dim(virt_energy, lax.axis_index("va") * rows, rows)
    eb = lax.dynamic_slice_in_dim(virt_energy, lax.axis_index("vb") * rows, rows)
    swap = [(0, 1), (1, 0)]
    vb = lax.axis_index("vb")
    table = jnp.concatenate([domain_blocks, pair_list[:, :1]], axis=1)
    both = jnp.stack([table, lax.ppermute(table, "pair", swap)])
    blocks, orbitals = both[:, :, :dom_blocks], both[:, :, dom_blocks]
    apart = (blocks // PER_OWNER) ^ vb
    apart_z, apart_y = apart // 4, apart % 4
    variant = blocks % PER_OWNER // 2
    near = jnp.where(variant == 0, 3, 1)
    code = jnp.where(
        apart_y == 0, 0, jnp.where(apart_y == near, 1, jnp.where(apart_y == 2, 3, 2))
    )
    inner = blocks % 2
    slots_high = (((apart_z * 2 + variant) * 4 + code) * 2 + inner) * SPLIT
    slots_low = (((variant * 4 + code) * 2 + apart_z) * 2 + inner) * SPLIT
    other_right = lax.ppermute(right_fit, "pair", swap)
    count = pairs // CHUNKS
    tiles = []
    for piece in range(CHUNKS):
        tiles += coulomb(left_fit, right_fit, piece * count, count, 1, tuple(tiles[-1:]))
    mirrors = []
    for piece, tile in enumerate(tiles):
        out, back = detour_pairs(piece)
        mid = lax.ppermute(tile, AXES, out)
        mirrors.append(lax.ppermute(mid, AXES, back))
    me = core.reshape(1).astype(jnp.int32)
    ready = (slots_high, slots_low, orbitals)
    keep, send = amplitude(me, occ_energy, pair_list, ea, eb, tiles, mirrors, ready)
    other_amp = lax.ppermute(send, "pair", swap)
    operands = (orbitals, keep, other_amp, right_fit, other_right)
    stay0, stay1, cross = contract(slots_high, *operands, SPLIT, (4, 4, 8))
    crossed = swap_z(cross)
    low0, sent0, low1, sent1 = contract(slots_low, *operands, 0, (4, 4, 4, 4))
    got0, got1 = step_y(sent0, 1), step_y(sent1, 3)
    kept_low, sent0, sent1 = add_halves(
        [(low0, 0), (low1, 0)], [(got0, 0), (got1, 0)], 4, False
    )
    got0, got1 = step_y(sent0, 3), step_y(sent1, 1)
    kept_high, high0, high1 = add_halves(
        [(stay0, 0), (stay1, 0)], [(crossed, 0), (crossed, 1)], 4, False
    )
    more0, more1 = step_y(high0, 1), step_y(high1, 3)
    kept_low, far = add_halves(
        [(kept_low, 0), (kept_low, 1)], [(got0, 0), (got1, 0)], 2, True
    )
    far = swap_z(far)
    kept_high, high0, high1 = add_halves(
        [(kept_high, 0), (kept_high, 1)], [(more0, 0), (more1, 0)], 2, False
    )
    high0, high1 = step_y(high0, 3), step_y(high1, 1)
    own, send = finish(me, kept_low, far, kept_high, high0, high1)
    return join(me, own, lax.ppermute(send, "pair", swap))


def solution(mesh):
    return jax.shard_map(
        program,
        mesh=mesh,
        in_specs=(
            P("pair", "va", None),
            P("pair", "vb", None),
            P(),
            P(),
            P("pair", None),
            P("pair", None),
        ),
        out_specs=P(("vb", "pair"), None, "va"),
        check_vma=False,
    )
```

```python
import itertools

import jax
import jax.numpy as jnp
from jax import lax
from jax.experimental import pallas as pl
from jax.experimental.pallas import tpu as pltpu
from jax.sharding import PartitionSpec as P


BLOCK = 128
AUX_BLK = 32
CHUNKS = 5
SPLIT = 4
PER_OWNER = 4
AXES = ("va", "vb", "pair")
DETOURS = (
    (0, 3, 3), (1, 3, 0), (0, 2, 3), (3, 0, 1), (0, 2, 1), (3, 1, 0), (0, 1, 1), (1, 0, 2), (2, 2, 0), (1, 0, 3),
)


def to_flat(x, y, z, core):
    va = x * 2 + z // 2
    vb = (z % 2) * 4 + y
    return (va * 8 + vb) * 2 + core


def mirror_chip(x, y, z):
    va, vb = x * 2 + z // 2, (z % 2) * 4 + y
    va, vb = vb, va
    return va // 2, vb % 4, (va % 2) * 2 + vb // 4


def detour_pairs(piece):
    out, back = [], []
    for x, y, z, core in itertools.product(range(4), range(4), range(4), range(2)):
        dx, dy, dz = DETOURS[core * CHUNKS + piece]
        mid = ((x + dx) % 4, (y + dy) % 4, (z + dz) % 4)
        out.append((to_flat(x, y, z, core), to_flat(*mid, core)))
        back.append((to_flat(*mid, core), to_flat(*mirror_chip(x, y, z), core)))
    return out, back


def coulomb_kernel(start, chunks, left_ref, right_ref, *refs):
    out_refs, (left_buf, right_buf, sems) = refs[-3 - chunks : -3], refs[-3:]
    count = out_refs[0].shape[0]
    copies = []
    for p in range(count * len(out_refs)):
        pair = [
            pltpu.make_async_copy(left_ref.at[start + p], left_buf.at[p], sems.at[0, p]),
            pltpu.make_async_copy(right_ref.at[start + p], right_buf.at[p], sems.at[1, p]),
        ]
        for copy in pair:
            copy.start()
        copies.append(pair)
    for p, pair in enumerate(copies):
        for copy in pair:
            copy.wait()
        out_refs[p // count][p % count] = lax.dot_general(
            left_buf[p], right_buf[p], (((1,), (1,)), ((), ())), preferred_element_type=jnp.float32
        ).astype(jnp.bfloat16)


def coulomb(left_fit, right_fit, start, count, chunks, after=()):
    _, rows, dom = left_fit.shape
    total = count * chunks
    hbm = pl.BlockSpec(memory_space=pl.ANY)
    return pl.pallas_call(
        lambda *refs: coulomb_kernel(start, chunks, *refs),
        in_specs=[hbm] * (2 + len(after)),
        out_specs=[pl.BlockSpec(memory_space=pltpu.VMEM)] * chunks,
        out_shape=[jax.ShapeDtypeStruct((count, rows, rows), jnp.bfloat16)] * chunks,
        scratch_shapes=[
            pltpu.VMEM((total, rows, dom), jnp.bfloat16),
            pltpu.VMEM((total, rows, dom), jnp.bfloat16),
            pltpu.SemaphoreType.DMA((2, total)),
        ],
        cost_estimate=pl.CostEstimate(
            flops=2 * total * rows * rows * dom,
            bytes_accessed=4 * total * rows * dom + 2 * total * rows * rows,
            transcendentals=0,
        ),
        compiler_params=pltpu.CompilerParams(vmem_limit_bytes=60 << 20),
        name="coulomb",
    )(left_fit, right_fit, *after)


def fetch(refs, buf_ref, sems):
    copies = [
        pltpu.make_async_copy(ref, buf_ref.at[n], sems.at[n]) for n, ref in enumerate(refs)
    ]
    for copy in copies:
        copy.start()
    return copies


def amplitude_kernel(chunks, *refs):
    core_ref, occ_ref, pair_ref = refs[:3]
    keep_ref, send_ref, work_ref, buf_ref, sems = refs[-5:]
    refs = refs[:-5]
    ea_ref, eb_ref = refs[-2 - 2 * chunks : -2 * chunks]
    copies = fetch(refs[-2 * chunks :], buf_ref, sems)
    tiles = [buf_ref.at[n] for n in range(chunks)]
    mirrors = [buf_ref.at[chunks + n] for n in range(chunks)]
    half = keep_ref.shape[1]
    count = tiles[0].shape[0]
    core = core_ref[0]
    base = ea_ref[...] + eb_ref[...]
    mine = pl.multiple_of(core * half, half)
    other = pl.multiple_of((1 - core) * half, half)
    for chunk in range(chunks):
        copies[chunk].wait()
        copies[chunks + chunk].wait()
        for row in range(count):
            p = chunk * count + row
            gap = base - occ_ref[pair_ref[p, 0]] - occ_ref[pair_ref[p, 1]]
            tile = tiles[chunk][row].astype(jnp.float32)
            swapped = mirrors[chunk][row].T.astype(jnp.float32)
            work_ref[p % 2] = ((2.0 * tile - swapped) / gap).astype(jnp.bfloat16)
            keep_ref[p] = work_ref[p % 2, pl.ds(mine, half), :]
            send_ref[p] = work_ref[p % 2, pl.ds(other, half), :]


def amplitude(core, occ_energy, pair_list, ea, eb, tiles, mirrors, ready):
    pairs = pair_list.shape[0]
    rows = tiles[0].shape[1]
    smem = pl.BlockSpec(memory_space=pltpu.SMEM)
    vmem = pl.BlockSpec(memory_space=pltpu.VMEM)
    hbm = pl.BlockSpec(memory_space=pl.ANY)
    chunks = len(tiles)
    shape = jax.ShapeDtypeStruct((pairs, rows // 2, rows), jnp.bfloat16)
    return pl.pallas_call(
        lambda *refs: amplitude_kernel(chunks, *refs),
        in_specs=[smem] * (3 + len(ready)) + [vmem] * 2 + [hbm] * (2 * chunks),
        out_specs=[vmem, vmem],
        out_shape=[shape, shape],
        scratch_shapes=[
            pltpu.VMEM((2, rows, rows), jnp.bfloat16),
            pltpu.VMEM((2 * chunks,) + tiles[0].shape, jnp.bfloat16),
            pltpu.SemaphoreType.DMA((2 * chunks,)),
        ],
        cost_estimate=pl.CostEstimate(
            flops=10 * pairs * rows * rows, bytes_accessed=6 * pairs * rows * rows, transcendentals=0
        ),
        name="amplitude",
    )(
        core, occ_energy, pair_list, *ready, ea.reshape(rows, 1), eb.reshape(1, rows), *tiles, *mirrors
    )


def contract_kernel(low, slot_ref, occ_ref, amp0, amp1, right0, right1, *refs):
    out_refs, (amp_ref, amp_sems, buf_ref, acc_ref, stage_ref, in_sems, out_sems) = refs[:-7], refs[-7:]
    pairs = amp0.shape[0]
    amps = fetch((amp0, amp1), amp_ref, amp_sems)
    dom_blocks = slot_ref.shape[2]
    sides = ((amp0, right0), (amp1, right1))

    def taken(side, p):
        return (occ_ref[side, p] >= low) & (occ_ref[side, p] < low + SPLIT)

    def load(side, p):
        return pltpu.make_async_copy(
            sides[side][1].at[p], buf_ref.at[side, p], in_sems.at[side, p]
        )

    for side in range(2):

        @pl.loop(0, pairs)
        def _(p):
            @pl.when(taken(side, p))
            def _():
                load(side, p).start()

    acc_ref[...] = jnp.zeros_like(acc_ref)
    for side in range(2):
        amps[side].wait()

        @pl.loop(0, pairs)
        def _(p):
            @pl.when(taken(side, p))
            def _():
                load(side, p).wait()
                part = jnp.dot(amp_ref[side, p], buf_ref[side, p], preferred_element_type=jnp.float32)
                for k in range(dom_blocks):
                    slot = slot_ref[side, p, k] + occ_ref[side, p] - low
                    acc_ref[slot] += part[:, k * BLOCK : (k + 1) * BLOCK]

    group = out_refs[0].shape[1]
    copies = []
    for out_ref in out_refs:
        for block in range(out_ref.shape[0]):
            place = len(copies)
            stage_ref[place] = acc_ref[place * group : (place + 1) * group].astype(stage_ref.dtype)
            copy = pltpu.make_async_copy(
                stage_ref.at[place], out_ref.at[block], out_sems.at[place]
            )
            copy.start()
            copies.append(copy)
    for copy in copies:
        copy.wait()


def contract(slots, orbitals, amp0, amp1, right0, right1, low, outs):
    pairs, half, rows = amp0.shape
    dom = right0.shape[2]
    total = AUX_BLK * SPLIT
    places = sum(outs)
    group = total // places
    smem = pl.BlockSpec(memory_space=pltpu.SMEM)
    hbm = pl.BlockSpec(memory_space=pl.ANY)
    return pl.pallas_call(
        lambda *refs: contract_kernel(low, *refs),
        in_specs=[smem, smem, hbm, hbm, hbm, hbm],
        out_specs=[hbm] * len(outs),
        out_shape=[jax.ShapeDtypeStruct((n, group, half, BLOCK), jnp.bfloat16) for n in outs],
        scratch_shapes=[
            pltpu.VMEM((2, pairs, half, rows), jnp.bfloat16),
            pltpu.SemaphoreType.DMA((2,)),
            pltpu.VMEM((2, pairs, rows, dom), jnp.bfloat16),
            pltpu.VMEM((total, half, BLOCK), jnp.float32),
            pltpu.VMEM((places, group, half, BLOCK), jnp.bfloat16),
            pltpu.SemaphoreType.DMA((2, pairs)),
            pltpu.SemaphoreType.DMA((places,)),
        ],
        cost_estimate=pl.CostEstimate(
            flops=2 * pairs * half * rows * dom,
            bytes_accessed=2 * pairs * rows * dom + 2 * total * half * BLOCK,
            transcendentals=0,
        ),
        compiler_params=pltpu.CompilerParams(vmem_limit_bytes=60 << 20),
        name="contract",
    )(slots, orbitals, amp0, amp1, right0, right1)


def add_kernel(places, own0, other0, own1, other1, *refs):
    outs, (own_buf, other_buf, kept_buf, sent_buf, in_sems, out_sems) = refs[:-6], refs[-6:]
    kept_ref, sent = outs[0], outs[1:]
    count = own_buf.shape[1]
    half = count // 2
    order = [(variant, n) for n in [*range(half, count), *range(half)] for variant in range(2)]
    loads = {}
    for variant, n in order:
        own, other = ((own0, other0), (own1, other1))[variant]
        own_at, other_at = places[2 * variant], places[2 * variant + 1]
        loads[variant, n] = [
            pltpu.make_async_copy(
                own.at[own_at * count + n], own_buf.at[variant, n], in_sems.at[0, variant, n]
            ),
            pltpu.make_async_copy(
                other.at[other_at * count + n], other_buf.at[variant, n], in_sems.at[1, variant, n]
            ),
        ]
        for copy in loads[variant, n]:
            copy.start()
    stores = []
    for variant, n in order:
        for copy in loads[variant, n]:
            copy.wait()
        total = own_buf[variant, n].astype(jnp.float32) + other_buf[variant, n].astype(jnp.float32)
        if n < half:
            kept_buf[variant, n] = total
            source, target = kept_buf.at[variant, n], kept_ref.at[variant, n]
        else:
            sent_buf[variant, n - half] = total.astype(jnp.bfloat16)
            source = sent_buf.at[variant, n - half]
            if len(sent) == 2:
                target = sent[variant].at[n - half]
            else:
                target = sent[0].at[variant * half + n - half]
        store = pltpu.make_async_copy(source, target, out_sems.at[variant, n])
        store.start()
        stores.append(store)
    for store in stores:
        store.wait()


def add_halves(owns, others, count, joined):
    group, half, width = owns[0][0].shape[-3:]
    flat = [pair for pairs in zip(owns, others) for pair in pairs]
    arrays = [array.reshape((-1, group, half, width)) for array, _ in flat]
    places = [at for _, at in flat]
    sent = [count] if joined else [count // 2] * 2
    hbm = pl.BlockSpec(memory_space=pl.ANY)
    return pl.pallas_call(
        lambda *refs: add_kernel(places, *refs),
        in_specs=[hbm] * 4,
        out_specs=[hbm] * (1 + len(sent)),
        out_shape=[jax.ShapeDtypeStruct((2, count // 2, group, half, width), jnp.float32)]
        + [jax.ShapeDtypeStruct((n, group, half, width), jnp.bfloat16) for n in sent],
        scratch_shapes=[
            pltpu.VMEM((2, count, group, half, width), arrays[0].dtype),
            pltpu.VMEM((2, count, group, half, width), arrays[1].dtype),
            pltpu.VMEM((2, count // 2, group, half, width), jnp.float32),
            pltpu.VMEM((2, count // 2, group, half, width), jnp.bfloat16),
            pltpu.SemaphoreType.DMA((2, 2, count)),
            pltpu.SemaphoreType.DMA((2, count)),
        ],
        cost_estimate=pl.CostEstimate(
            flops=2 * count * group * half * width,
            bytes_accessed=14 * count * group * half * width,
            transcendentals=0,
        ),
        name="add_halves",
    )(*arrays)


def last_add_kernel(core_ref, kept_in, other0, other1, *refs):
    outs, (kept_buf, other_buf, sum_buf, sent_buf, in_sems, out_sems) = refs[:4], refs[4:]
    core = core_ref[0]
    loads = []
    for variant, other in enumerate((other0, other1)):
        loads.append(
            [
                pltpu.make_async_copy(
                    kept_in.at[variant], kept_buf.at[variant], in_sems.at[0, variant]
                ),
                pltpu.make_async_copy(other, other_buf.at[variant], in_sems.at[1, variant]),
            ]
        )
        for copy in loads[variant]:
            copy.start()
    for variant in range(2):
        for copy in loads[variant]:
            copy.wait()
        sent_buf[variant] = (
            kept_buf[variant, 1] + other_buf[variant, 1].astype(jnp.float32)
        ).astype(jnp.bfloat16)
        sum_buf[variant] = kept_buf[variant, 0] + other_buf[variant, 0].astype(jnp.float32)

    def stores(where):
        own_ref, swap_ref, same_ref, cross_ref = outs
        return [
            pltpu.make_async_copy(sent_buf.at[where], same_ref, out_sems.at[0]),
            pltpu.make_async_copy(sent_buf.at[1 - where], cross_ref, out_sems.at[1]),
            pltpu.make_async_copy(sum_buf.at[where], own_ref, out_sems.at[2]),
            pltpu.make_async_copy(sum_buf.at[1 - where], swap_ref, out_sems.at[3]),
        ]

    for where in range(2):

        @pl.when(core == where)
        def _():
            for copy in stores(where):
                copy.start()
            for copy in stores(where):
                copy.wait()


def last_add(core, kept, other0, other1):
    group, half, width = kept.shape[-3:]
    shape = (group, half, width)
    hbm = pl.BlockSpec(memory_space=pl.ANY)
    return pl.pallas_call(
        last_add_kernel,
        in_specs=[pl.BlockSpec(memory_space=pltpu.SMEM)] + [hbm] * 3,
        out_specs=[hbm] * 4,
        out_shape=[jax.ShapeDtypeStruct(shape, jnp.float32)] * 2
        + [jax.ShapeDtypeStruct(shape, jnp.bfloat16)] * 2,
        scratch_shapes=[
            pltpu.VMEM((2, 2) + shape, jnp.float32),
            pltpu.VMEM((2, 2) + shape, jnp.bfloat16),
            pltpu.VMEM((2,) + shape, jnp.float32),
            pltpu.VMEM((2,) + shape, jnp.bfloat16),
            pltpu.SemaphoreType.DMA((2, 2)),
            pltpu.SemaphoreType.DMA((4,)),
        ],
        cost_estimate=pl.CostEstimate(
            flops=kept.size, bytes_accessed=10 * kept.size, transcendentals=0
        ),
        name="last_add",
    )(core, kept, other0, other1)


def finish_kernel(core_ref, *refs):
    ins, (out_ref, kept_buf, far_buf, out_buf, in_sems, out_sems) = refs[:8], refs[8:]
    core = core_ref[0]
    blocks = PER_OWNER // 2
    half = kept_buf.shape[-2]
    loads = []
    for part in range(2):
        for side in range(2):
            at = 2 * part + side
            loads += [
                pltpu.make_async_copy(ins[4 * part + side], kept_buf.at[at], in_sems.at[0, at]),
                pltpu.make_async_copy(ins[4 * part + 2 + side], far_buf.at[at], in_sems.at[1, at]),
            ]
    for copy in loads:
        copy.start()
    for copy in loads:
        copy.wait()

    def write(block, order):
        rows = slice(block * BLOCK, (block + 1) * BLOCK)
        for part in range(2):
            for occ in range(SPLIT):
                row = block * SPLIT + occ
                for side in range(2):
                    at = 2 * part + (side if order == 0 else 1 - side)
                    total = kept_buf[at, row] + far_buf[at, row].astype(jnp.float32)
                    out_buf[rows, part * SPLIT + occ, side * half : (side + 1) * half] = total.T

    stores = []
    for block in range(blocks):

        @pl.when(core == 0)
        def _():
            write(block, 0)

        @pl.when(core != 0)
        def _():
            write(block, 1)

        rows = slice(block * BLOCK, (block + 1) * BLOCK)
        store = pltpu.make_async_copy(out_buf.at[rows], out_ref.at[rows], out_sems.at[block])
        store.start()
        stores.append(store)
    for store in stores:
        store.wait()


def finish(core, low, high):
    group, half, width = low[0].shape
    blocks = PER_OWNER // 2
    hbm = pl.BlockSpec(memory_space=pl.ANY)
    shape = jax.ShapeDtypeStruct((blocks * width, 2 * SPLIT, 2 * half), jnp.float32)
    return pl.pallas_call(
        finish_kernel,
        in_specs=[pl.BlockSpec(memory_space=pltpu.SMEM)] + [hbm] * 8,
        out_specs=hbm,
        out_shape=shape,
        scratch_shapes=[
            pltpu.VMEM((4, group, half, width), jnp.float32),
            pltpu.VMEM((4, group, half, width), jnp.bfloat16),
            pltpu.VMEM(shape.shape, jnp.float32),
            pltpu.SemaphoreType.DMA((2, 4)),
            pltpu.SemaphoreType.DMA((blocks,)),
        ],
        cost_estimate=pl.CostEstimate(
            flops=shape.size, bytes_accessed=10 * shape.size, transcendentals=0
        ),
        name="finish",
    )(core, *low, *high)


def last_steps(same, cross, bits):
    pairs_same, pairs_cross = [], []
    for vb, core in itertools.product(range(8), range(2)):
        pairs_same.append((vb * 2 + core, (vb ^ bits[core]) * 2 + core))
        pairs_cross.append((vb * 2 + core, (vb ^ bits[1 - core]) * 2 + 1 - core))
    axes = ("vb", "pair")
    return lax.ppermute(same, axes, pairs_same), lax.ppermute(cross, axes, pairs_cross)


def step_y(value, bits):
    return lax.ppermute(value, "vb", [(j, j ^ bits) for j in range(8)])


def swap_z(value):
    return step_y(value, 4)


def program(left_fit, right_fit, occ_energy, virt_energy, pair_list, domain_blocks):
    pairs, rows, _ = left_fit.shape
    dom_blocks = domain_blocks.shape[1]
    core = lax.axis_index("pair")
    ea = lax.dynamic_slice_in_dim(virt_energy, lax.axis_index("va") * rows, rows)
    eb = lax.dynamic_slice_in_dim(virt_energy, lax.axis_index("vb") * rows, rows)
    swap = [(0, 1), (1, 0)]
    vb = lax.axis_index("vb")
    table = jnp.concatenate([domain_blocks, pair_list[:, :1]], axis=1)
    both = jnp.stack([table, lax.ppermute(table, "pair", swap)])
    blocks, orbitals = both[:, :, :dom_blocks], both[:, :, dom_blocks]
    apart = (blocks // PER_OWNER) ^ vb
    apart_z, apart_y = apart // 4, apart % 4
    variant = blocks % PER_OWNER // 2
    near = jnp.where(variant == 0, 3, 1)
    code = jnp.where(
        apart_y == 0, 0, jnp.where(apart_y == near, 1, jnp.where(apart_y == 2, 3, 2))
    )
    inner = blocks % 2
    slots_high = (((apart_z * 2 + variant) * 4 + code) * 2 + inner) * SPLIT
    slots_low = (((variant * 4 + code) * 2 + apart_z) * 2 + inner) * SPLIT
    other_right = lax.ppermute(right_fit, "pair", swap)
    count = pairs // CHUNKS
    tiles = []
    for piece in range(CHUNKS):
        tiles += coulomb(left_fit, right_fit, piece * count, count, 1, tuple(tiles[-1:]))
    mirrors = []
    for piece, tile in enumerate(tiles):
        out, back = detour_pairs(piece)
        mid = lax.ppermute(tile, AXES, out)
        mirrors.append(lax.ppermute(mid, AXES, back))
    me = core.reshape(1).astype(jnp.int32)
    ready = (slots_high, slots_low, orbitals)
    keep, send = amplitude(me, occ_energy, pair_list, ea, eb, tiles, mirrors, ready)
    other_amp = lax.ppermute(send, "pair", swap)
    operands = (orbitals, keep, other_amp, right_fit, other_right)
    stay0, stay1, cross = contract(slots_high, *operands, SPLIT, (4, 4, 8))
    crossed = swap_z(cross)
    low0, sent0, low1, sent1 = contract(slots_low, *operands, 0, (4, 4, 4, 4))
    got0, got1 = step_y(sent0, 1), step_y(sent1, 3)
    kept_low, sent0, sent1 = add_halves(
        [(low0, 0), (low1, 0)], [(got0, 0), (got1, 0)], 4, False
    )
    got0, got1 = step_y(sent0, 3), step_y(sent1, 1)
    kept_high, high0, high1 = add_halves(
        [(stay0, 0), (stay1, 0)], [(crossed, 0), (crossed, 1)], 4, False
    )
    more0, more1 = step_y(high0, 1), step_y(high1, 3)
    own_low, swap_low, *sent = last_add(me, kept_low, got0, got1)
    arrived = last_steps(*sent, (4, 4))
    low = [own_low, lax.ppermute(swap_low, "pair", swap), *arrived]
    own_high, swap_high, *sent = last_add(me, kept_high, more0, more1)
    high = [own_high, lax.ppermute(swap_high, "pair", swap), *last_steps(*sent, (3, 1))]
    return finish(me, low, high)


def solution(mesh):
    return jax.shard_map(
        program,
        mesh=mesh,
        in_specs=(
            P("pair", "va", None),
            P("pair", "vb", None),
            P(),
            P(),
            P("pair", None),
            P("pair", None),
        ),
        out_specs=P(("vb", "pair"), None, "va"),
        check_vma=False,
    )
```

```python
import itertools

import jax
import jax.numpy as jnp
from jax import lax
from jax.experimental import pallas as pl
from jax.experimental.pallas import tpu as pltpu
from jax.sharding import PartitionSpec as P


BLOCK = 128
AUX_BLK = 32
CHUNKS = 5
SPLIT = 4
PER_OWNER = 4
AXES = ("va", "vb", "pair")
DETOURS = (
    (0, 3, 3), (1, 3, 0), (0, 2, 3), (3, 0, 1), (0, 2, 1), (3, 1, 0), (0, 1, 1), (1, 0, 2), (2, 2, 0), (1, 0, 3),
)


def to_flat(x, y, z, core):
    va = x * 2 + z // 2
    vb = (z % 2) * 4 + y
    return (va * 8 + vb) * 2 + core


def mirror_chip(x, y, z):
    va, vb = x * 2 + z // 2, (z % 2) * 4 + y
    va, vb = vb, va
    return va // 2, vb % 4, (va % 2) * 2 + vb // 4


def detour_pairs(piece):
    out, back = [], []
    for x, y, z, core in itertools.product(range(4), range(4), range(4), range(2)):
        dx, dy, dz = DETOURS[core * CHUNKS + piece]
        mid = ((x + dx) % 4, (y + dy) % 4, (z + dz) % 4)
        out.append((to_flat(x, y, z, core), to_flat(*mid, core)))
        back.append((to_flat(*mid, core), to_flat(*mirror_chip(x, y, z), core)))
    return out, back


def coulomb_kernel(start, chunks, left_ref, right_ref, *refs):
    out_refs, (left_buf, right_buf, sems) = refs[-3 - chunks : -3], refs[-3:]
    count = out_refs[0].shape[0]
    copies = []
    for p in range(count * len(out_refs)):
        pair = [
            pltpu.make_async_copy(left_ref.at[start + p], left_buf.at[p], sems.at[0, p]),
            pltpu.make_async_copy(right_ref.at[start + p], right_buf.at[p], sems.at[1, p]),
        ]
        for copy in pair:
            copy.start()
        copies.append(pair)
    for p, pair in enumerate(copies):
        for copy in pair:
            copy.wait()
        out_refs[p // count][p % count] = lax.dot_general(
            left_buf[p], right_buf[p], (((1,), (1,)), ((), ())), preferred_element_type=jnp.float32
        ).astype(jnp.bfloat16)


def coulomb(left_fit, right_fit, start, count, chunks, after=()):
    _, rows, dom = left_fit.shape
    total = count * chunks
    hbm = pl.BlockSpec(memory_space=pl.ANY)
    return pl.pallas_call(
        lambda *refs: coulomb_kernel(start, chunks, *refs),
        in_specs=[hbm] * (2 + len(after)),
        out_specs=[pl.BlockSpec(memory_space=pltpu.VMEM)] * chunks,
        out_shape=[jax.ShapeDtypeStruct((count, rows, rows), jnp.bfloat16)] * chunks,
        scratch_shapes=[
            pltpu.VMEM((total, rows, dom), jnp.bfloat16),
            pltpu.VMEM((total, rows, dom), jnp.bfloat16),
            pltpu.SemaphoreType.DMA((2, total)),
        ],
        cost_estimate=pl.CostEstimate(
            flops=2 * total * rows * rows * dom,
            bytes_accessed=4 * total * rows * dom + 2 * total * rows * rows,
            transcendentals=0,
        ),
        compiler_params=pltpu.CompilerParams(vmem_limit_bytes=60 << 20),
        name="coulomb",
    )(left_fit, right_fit, *after)


def fetch(refs, buf_ref, sems):
    copies = [
        pltpu.make_async_copy(ref, buf_ref.at[n], sems.at[n]) for n, ref in enumerate(refs)
    ]
    for copy in copies:
        copy.start()
    return copies


def amplitude_kernel(chunks, *refs):
    core_ref, occ_ref, pair_ref = refs[:3]
    keep_ref, send_ref, work_ref, buf_ref, sems = refs[-5:]
    refs = refs[:-5]
    ea_ref, eb_ref = refs[-2 - 2 * chunks : -2 * chunks]
    copies = fetch(refs[-2 * chunks :], buf_ref, sems)
    tiles = [buf_ref.at[n] for n in range(chunks)]
    mirrors = [buf_ref.at[chunks + n] for n in range(chunks)]
    half = keep_ref.shape[1]
    count = tiles[0].shape[0]
    core = core_ref[0]
    base = ea_ref[...] + eb_ref[...]
    mine = pl.multiple_of(core * half, half)
    other = pl.multiple_of((1 - core) * half, half)
    for chunk in range(chunks):
        copies[chunk].wait()
        copies[chunks + chunk].wait()
        for row in range(count):
            p = chunk * count + row
            gap = base - occ_ref[pair_ref[p, 0]] - occ_ref[pair_ref[p, 1]]
            tile = tiles[chunk][row].astype(jnp.float32)
            swapped = mirrors[chunk][row].astype(jnp.float32).T
            work_ref[p % 2] = ((2.0 * tile - swapped) / gap).astype(jnp.bfloat16)
            keep_ref[p] = work_ref[p % 2, pl.ds(mine, half), :]
            send_ref[p] = work_ref[p % 2, pl.ds(other, half), :]


def amplitude(core, occ_energy, pair_list, ea, eb, tiles, mirrors, ready):
    pairs = pair_list.shape[0]
    rows = tiles[0].shape[1]
    smem = pl.BlockSpec(memory_space=pltpu.SMEM)
    vmem = pl.BlockSpec(memory_space=pltpu.VMEM)
    hbm = pl.BlockSpec(memory_space=pl.ANY)
    chunks = len(tiles)
    shape = jax.ShapeDtypeStruct((pairs, rows // 2, rows), jnp.bfloat16)
    return pl.pallas_call(
        lambda *refs: amplitude_kernel(chunks, *refs),
        in_specs=[smem] * (3 + len(ready)) + [vmem] * 2 + [hbm] * (2 * chunks),
        out_specs=[vmem, vmem],
        out_shape=[shape, shape],
        scratch_shapes=[
            pltpu.VMEM((2, rows, rows), jnp.bfloat16),
            pltpu.VMEM((2 * chunks,) + tiles[0].shape, jnp.bfloat16),
            pltpu.SemaphoreType.DMA((2 * chunks,)),
        ],
        cost_estimate=pl.CostEstimate(
            flops=10 * pairs * rows * rows, bytes_accessed=6 * pairs * rows * rows, transcendentals=0
        ),
        name="amplitude",
    )(
        core, occ_energy, pair_list, *ready, ea.reshape(rows, 1), eb.reshape(1, rows), *tiles, *mirrors
    )


def contract_kernel(low, slot_ref, occ_ref, amp0, amp1, right0, right1, *refs):
    out_refs, (amp_ref, amp_sems, buf_ref, acc_ref, stage_ref, in_sems, out_sems) = refs[:-7], refs[-7:]
    pairs = amp0.shape[0]
    amps = fetch((amp0, amp1), amp_ref, amp_sems)
    dom_blocks = slot_ref.shape[2]
    sides = ((amp0, right0), (amp1, right1))

    def taken(side, p):
        return (occ_ref[side, p] >= low) & (occ_ref[side, p] < low + SPLIT)

    def load(side, p):
        return pltpu.make_async_copy(
            sides[side][1].at[p], buf_ref.at[side, p], in_sems.at[side, p]
        )

    for side in range(2):

        @pl.loop(0, pairs)
        def _(p):
            @pl.when(taken(side, p))
            def _():
                load(side, p).start()

    acc_ref[...] = jnp.zeros_like(acc_ref)
    for side in range(2):
        amps[side].wait()

        @pl.loop(0, pairs)
        def _(p):
            @pl.when(taken(side, p))
            def _():
                load(side, p).wait()
                part = jnp.dot(amp_ref[side, p], buf_ref[side, p], preferred_element_type=jnp.float32)
                for k in range(dom_blocks):
                    slot = slot_ref[side, p, k] + occ_ref[side, p] - low
                    acc_ref[slot] += part[:, k * BLOCK : (k + 1) * BLOCK]

    group = out_refs[0].shape[1]
    copies = []
    for out_ref in out_refs:
        for block in range(out_ref.shape[0]):
            place = len(copies)
            stage_ref[place] = acc_ref[place * group : (place + 1) * group].astype(stage_ref.dtype)
            copy = pltpu.make_async_copy(
                stage_ref.at[place], out_ref.at[block], out_sems.at[place]
            )
            copy.start()
            copies.append(copy)
    for copy in copies:
        copy.wait()


def contract(slots, orbitals, amp0, amp1, right0, right1, low, outs):
    pairs, half, rows = amp0.shape
    dom = right0.shape[2]
    total = AUX_BLK * SPLIT
    places = sum(outs)
    group = total // places
    smem = pl.BlockSpec(memory_space=pltpu.SMEM)
    hbm = pl.BlockSpec(memory_space=pl.ANY)
    return pl.pallas_call(
        lambda *refs: contract_kernel(low, *refs),
        in_specs=[smem, smem, hbm, hbm, hbm, hbm],
        out_specs=[hbm] * len(outs),
        out_shape=[jax.ShapeDtypeStruct((n, group, half, BLOCK), jnp.bfloat16) for n in outs],
        scratch_shapes=[
            pltpu.VMEM((2, pairs, half, rows), jnp.bfloat16),
            pltpu.SemaphoreType.DMA((2,)),
            pltpu.VMEM((2, pairs, rows, dom), jnp.bfloat16),
            pltpu.VMEM((total, half, BLOCK), jnp.float32),
            pltpu.VMEM((places, group, half, BLOCK), jnp.bfloat16),
            pltpu.SemaphoreType.DMA((2, pairs)),
            pltpu.SemaphoreType.DMA((places,)),
        ],
        cost_estimate=pl.CostEstimate(
            flops=2 * pairs * half * rows * dom,
            bytes_accessed=2 * pairs * rows * dom + 2 * total * half * BLOCK,
            transcendentals=0,
        ),
        compiler_params=pltpu.CompilerParams(vmem_limit_bytes=60 << 20),
        name="contract",
    )(slots, orbitals, amp0, amp1, right0, right1)


def add_kernel(places, own0, other0, own1, other1, *refs):
    outs, (own_buf, other_buf, kept_buf, sent_buf, in_sems, out_sems) = refs[:-6], refs[-6:]
    kept_ref, sent = outs[0], outs[1:]
    count = own_buf.shape[1]
    half = count // 2
    order = [(variant, n) for n in [*range(half, count), *range(half)] for variant in range(2)]
    loads = {}
    for variant, n in order:
        own, other = ((own0, other0), (own1, other1))[variant]
        own_at, other_at = places[2 * variant], places[2 * variant + 1]
        loads[variant, n] = [
            pltpu.make_async_copy(
                own.at[own_at * count + n], own_buf.at[variant, n], in_sems.at[0, variant, n]
            ),
            pltpu.make_async_copy(
                other.at[other_at * count + n], other_buf.at[variant, n], in_sems.at[1, variant, n]
            ),
        ]
        for copy in loads[variant, n]:
            copy.start()
    stores = []
    for variant, n in order:
        for copy in loads[variant, n]:
            copy.wait()
        total = own_buf[variant, n].astype(jnp.float32) + other_buf[variant, n].astype(jnp.float32)
        if n < half:
            kept_buf[variant, n] = total
            source, target = kept_buf.at[variant, n], kept_ref.at[variant, n]
        else:
            sent_buf[variant, n - half] = total.astype(jnp.bfloat16)
            source = sent_buf.at[variant, n - half]
            if len(sent) == 2:
                target = sent[variant].at[n - half]
            else:
                target = sent[0].at[variant * half + n - half]
        store = pltpu.make_async_copy(source, target, out_sems.at[variant, n])
        store.start()
        stores.append(store)
    for store in stores:
        store.wait()


def add_halves(owns, others, count, joined):
    group, half, width = owns[0][0].shape[-3:]
    flat = [pair for pairs in zip(owns, others) for pair in pairs]
    arrays = [array.reshape((-1, group, half, width)) for array, _ in flat]
    places = [at for _, at in flat]
    sent = [count] if joined else [count // 2] * 2
    hbm = pl.BlockSpec(memory_space=pl.ANY)
    return pl.pallas_call(
        lambda *refs: add_kernel(places, *refs),
        in_specs=[hbm] * 4,
        out_specs=[hbm] * (1 + len(sent)),
        out_shape=[jax.ShapeDtypeStruct((2, count // 2, group, half, width), jnp.float32)]
        + [jax.ShapeDtypeStruct((n, group, half, width), jnp.bfloat16) for n in sent],
        scratch_shapes=[
            pltpu.VMEM((2, count, group, half, width), arrays[0].dtype),
            pltpu.VMEM((2, count, group, half, width), arrays[1].dtype),
            pltpu.VMEM((2, count // 2, group, half, width), jnp.float32),
            pltpu.VMEM((2, count // 2, group, half, width), jnp.bfloat16),
            pltpu.SemaphoreType.DMA((2, 2, count)),
            pltpu.SemaphoreType.DMA((2, count)),
        ],
        cost_estimate=pl.CostEstimate(
            flops=2 * count * group * half * width,
            bytes_accessed=14 * count * group * half * width,
            transcendentals=0,
        ),
        name="add_halves",
    )(*arrays)


def last_add_kernel(core_ref, kept_in, other0, other1, *refs):
    outs, (kept_buf, other_buf, sum_buf, sent_buf, in_sems, out_sems) = refs[:4], refs[4:]
    core = core_ref[0]
    loads = []
    for variant, other in enumerate((other0, other1)):
        loads.append(
            [
                pltpu.make_async_copy(
                    kept_in.at[variant], kept_buf.at[variant], in_sems.at[0, variant]
                ),
                pltpu.make_async_copy(other, other_buf.at[variant], in_sems.at[1, variant]),
            ]
        )
        for copy in loads[variant]:
            copy.start()
    for variant in range(2):
        for copy in loads[variant]:
            copy.wait()
        sent_buf[variant] = (
            kept_buf[variant, 1] + other_buf[variant, 1].astype(jnp.float32)
        ).astype(jnp.bfloat16)
        sum_buf[variant] = kept_buf[variant, 0] + other_buf[variant, 0].astype(jnp.float32)

    def stores(where):
        own_ref, swap_ref, same_ref, cross_ref = outs
        return [
            pltpu.make_async_copy(sent_buf.at[where], same_ref, out_sems.at[0]),
            pltpu.make_async_copy(sent_buf.at[1 - where], cross_ref, out_sems.at[1]),
            pltpu.make_async_copy(sum_buf.at[where], own_ref, out_sems.at[2]),
            pltpu.make_async_copy(sum_buf.at[1 - where], swap_ref, out_sems.at[3]),
        ]

    for where in range(2):

        @pl.when(core == where)
        def _():
            for copy in stores(where):
                copy.start()
            for copy in stores(where):
                copy.wait()


def last_add(core, kept, other0, other1):
    group, half, width = kept.shape[-3:]
    shape = (group, half, width)
    hbm = pl.BlockSpec(memory_space=pl.ANY)
    return pl.pallas_call(
        last_add_kernel,
        in_specs=[pl.BlockSpec(memory_space=pltpu.SMEM)] + [hbm] * 3,
        out_specs=[hbm] * 4,
        out_shape=[jax.ShapeDtypeStruct(shape, jnp.float32)] * 2
        + [jax.ShapeDtypeStruct(shape, jnp.bfloat16)] * 2,
        scratch_shapes=[
            pltpu.VMEM((2, 2) + shape, jnp.float32),
            pltpu.VMEM((2, 2) + shape, jnp.bfloat16),
            pltpu.VMEM((2,) + shape, jnp.float32),
            pltpu.VMEM((2,) + shape, jnp.bfloat16),
            pltpu.SemaphoreType.DMA((2, 2)),
            pltpu.SemaphoreType.DMA((4,)),
        ],
        cost_estimate=pl.CostEstimate(
            flops=kept.size, bytes_accessed=10 * kept.size, transcendentals=0
        ),
        name="last_add",
    )(core, kept, other0, other1)


def finish_kernel(core_ref, *refs):
    ins, (out_ref, kept_buf, far_buf, out_buf, in_sems, out_sems) = refs[:8], refs[8:]
    core = core_ref[0]
    blocks = PER_OWNER // 2
    half = kept_buf.shape[-2]
    loads = []
    for block in range(blocks):
        rows = slice(block * SPLIT, (block + 1) * SPLIT)
        for at in range(4):
            kept, far = ins[at // 2 * 4 + at % 2], ins[at // 2 * 4 + 2 + at % 2]
            loads += [
                pltpu.make_async_copy(
                    kept.at[rows], kept_buf.at[at, rows], in_sems.at[0, at, block]
                ),
                pltpu.make_async_copy(far.at[rows], far_buf.at[at, rows], in_sems.at[1, at, block]),
            ]
    for copy in loads:
        copy.start()

    def write(block, order):
        rows = slice(block * BLOCK, (block + 1) * BLOCK)
        for part in range(2):
            for occ in range(SPLIT):
                row = block * SPLIT + occ
                for side in range(2):
                    at = 2 * part + (side if order == 0 else 1 - side)
                    total = kept_buf[at, row] + far_buf[at, row].astype(jnp.float32)
                    out_buf[rows, part * SPLIT + occ, side * half : (side + 1) * half] = total.T

    stores = []
    for block in range(blocks):
        for copy in loads[block * 8 : (block + 1) * 8]:
            copy.wait()

        @pl.when(core == 0)
        def _():
            write(block, 0)

        @pl.when(core != 0)
        def _():
            write(block, 1)

        rows = slice(block * BLOCK, (block + 1) * BLOCK)
        store = pltpu.make_async_copy(out_buf.at[rows], out_ref.at[rows], out_sems.at[block])
        store.start()
        stores.append(store)
    for store in stores:
        store.wait()


def finish(core, low, high):
    group, half, width = low[0].shape
    blocks = PER_OWNER // 2
    hbm = pl.BlockSpec(memory_space=pl.ANY)
    shape = jax.ShapeDtypeStruct((blocks * width, 2 * SPLIT, 2 * half), jnp.float32)
    return pl.pallas_call(
        finish_kernel,
        in_specs=[pl.BlockSpec(memory_space=pltpu.SMEM)] + [hbm] * 8,
        out_specs=hbm,
        out_shape=shape,
        scratch_shapes=[
            pltpu.VMEM((4, group, half, width), jnp.float32),
            pltpu.VMEM((4, group, half, width), jnp.bfloat16),
            pltpu.VMEM(shape.shape, jnp.float32),
            pltpu.SemaphoreType.DMA((2, 4, blocks)),
            pltpu.SemaphoreType.DMA((blocks,)),
        ],
        cost_estimate=pl.CostEstimate(
            flops=shape.size, bytes_accessed=10 * shape.size, transcendentals=0
        ),
        name="finish",
    )(core, *low, *high)


def last_steps(same, cross, bits):
    pairs_same, pairs_cross = [], []
    for vb, core in itertools.product(range(8), range(2)):
        pairs_same.append((vb * 2 + core, (vb ^ bits[core]) * 2 + core))
        pairs_cross.append((vb * 2 + core, (vb ^ bits[1 - core]) * 2 + 1 - core))
    axes = ("vb", "pair")
    return lax.ppermute(same, axes, pairs_same), lax.ppermute(cross, axes, pairs_cross)


def step_y(value, bits):
    return lax.ppermute(value, "vb", [(j, j ^ bits) for j in range(8)])


def swap_z(value):
    return step_y(value, 4)


def program(left_fit, right_fit, occ_energy, virt_energy, pair_list, domain_blocks):
    pairs, rows, _ = left_fit.shape
    dom_blocks = domain_blocks.shape[1]
    core = lax.axis_index("pair")
    ea = lax.dynamic_slice_in_dim(virt_energy, lax.axis_index("va") * rows, rows)
    eb = lax.dynamic_slice_in_dim(virt_energy, lax.axis_index("vb") * rows, rows)
    swap = [(0, 1), (1, 0)]
    vb = lax.axis_index("vb")
    table = jnp.concatenate([domain_blocks, pair_list[:, :1]], axis=1)
    both = jnp.stack([table, lax.ppermute(table, "pair", swap)])
    blocks, orbitals = both[:, :, :dom_blocks], both[:, :, dom_blocks]
    apart = (blocks // PER_OWNER) ^ vb
    apart_z, apart_y = apart // 4, apart % 4
    variant = blocks % PER_OWNER // 2
    near = jnp.where(variant == 0, 3, 1)
    code = jnp.where(
        apart_y == 0, 0, jnp.where(apart_y == near, 1, jnp.where(apart_y == 2, 3, 2))
    )
    inner = blocks % 2
    slots_high = (((apart_z * 2 + variant) * 4 + code) * 2 + inner) * SPLIT
    slots_low = (((variant * 4 + code) * 2 + apart_z) * 2 + inner) * SPLIT
    other_right = lax.ppermute(right_fit, "pair", swap)
    count = pairs // CHUNKS
    tiles = []
    for piece in range(CHUNKS):
        tiles += coulomb(left_fit, right_fit, piece * count, count, 1, tuple(tiles[-1:]))
    mirrors = []
    for piece, tile in enumerate(tiles):
        out, back = detour_pairs(piece)
        mid = lax.ppermute(tile, AXES, out)
        mirrors.append(lax.ppermute(mid, AXES, back))
    me = core.reshape(1).astype(jnp.int32)
    ready = (slots_high, slots_low, orbitals)
    keep, send = amplitude(me, occ_energy, pair_list, ea, eb, tiles, mirrors, ready)
    other_amp = lax.ppermute(send, "pair", swap)
    operands = (orbitals, keep, other_amp, right_fit, other_right)
    stay0, stay1, cross = contract(slots_high, *operands, SPLIT, (4, 4, 8))
    crossed = swap_z(cross)
    low0, sent0, low1, sent1 = contract(slots_low, *operands, 0, (4, 4, 4, 4))
    got0, got1 = step_y(sent0, 1), step_y(sent1, 3)
    kept_low, sent0, sent1 = add_halves(
        [(low0, 0), (low1, 0)], [(got0, 0), (got1, 0)], 4, False
    )
    got0, got1 = step_y(sent0, 3), step_y(sent1, 1)
    kept_high, high0, high1 = add_halves(
        [(stay0, 0), (stay1, 0)], [(crossed, 0), (crossed, 1)], 4, False
    )
    more0, more1 = step_y(high0, 1), step_y(high1, 3)
    own_low, swap_low, *sent = last_add(me, kept_low, got0, got1)
    arrived = last_steps(*sent, (4, 4))
    low = [own_low, lax.ppermute(swap_low, "pair", swap), *arrived]
    own_high, swap_high, *sent = last_add(me, kept_high, more0, more1)
    high = [own_high, lax.ppermute(swap_high, "pair", swap), *last_steps(*sent, (3, 1))]
    return finish(me, low, high)


def solution(mesh):
    return jax.shard_map(
        program,
        mesh=mesh,
        in_specs=(
            P("pair", "va", None),
            P("pair", "vb", None),
            P(),
            P(),
            P("pair", None),
            P("pair", None),
        ),
        out_specs=P(("vb", "pair"), None, "va"),
        check_vma=False,
    )
```
